128 devices in a mesh: loop: 8 (over z_lo, y), wide: 16 (over z_hi, x, core).
Axes of the slice: x: 4, y: 4, z: 4 (z_hi: 2, z_lo: 2; z = z_hi * 2 + z_lo), core: 2. Of those that a mesh axis runs over, the one named last changes fastest.
Arguments:
- feats: bfloat16 [16, 2048, 256], P('wide', 'loop'), may hold values from -6 to 6
- w_first: bfloat16 [256, 1024], replicated, may hold values from -0.375 to 0.375
- w_second: bfloat16 [1024, 256], replicated, may hold values from -0.1875 to 0.1875
- cotangent: bfloat16 [16, 2048, 256], P('wide', 'loop'), may hold values from -0.078125 to 0.078125
- block_values: bfloat16 [8, 16, 80, 64, 64], P('loop', 'wide'), may hold values from -0.25 to 0.25
- row_ptr: int32 [8, 16, 33], P('loop', 'wide'), may hold values from 0 to 80, as said below
- col_idx: int32 [8, 16, 80], P('loop', 'wide'), may hold values from 0 to 63
Outputs:
- propagated: bfloat16 [16, 2048, 256], P('wide', 'loop')
- grad_first: float32 [256, 1024], P('wide')
- grad_second: float32 [1024, 256], P('wide')
The draws below stay inside these ranges and needn't reach their ends.
Inputs may be any that keep to these rules, and one draw needn't show every extreme that they name: In each tile row_ptr starts at 0, never falls, and its last entry (the tile's live blocks) is at most 80; in every draw some tile has exactly 80 live blocks. `col_idx`: entries of empty slots are ignored.
All inputs are finite; a program needn't handle non-finite values.
Results may differ from the reference program's by a relative error of at most 0.02.
Values may be sent and summed in bfloat16 or wider, within the bound.
No kernel may reach another device: no remote copies, remote signals or barrier semaphores. Data moves between devices by JAX's collectives and lax.ppermute only.
A program may use at most 128 MiB of HBM per device.

```python
import jax
import jax.numpy as jnp
from jax import lax

D = 256
HID = 1024
BLK = 64
BPR = 8
STEPS = 3
ITEMS_DEV = 256
SLOTS = 80
ROWS_W = 2048
ROWBLK = 32
COLBLK = 64
ITEMS = 32768
N_LOOP = 8
N_WIDE = 16


def draw_row_ptr(key, part):
    key_count, key_hot, key_pick, key_rows = jax.random.split(jax.random.fold_in(key, 17), 4)
    tile_total = N_LOOP * N_WIDE
    counts = jax.random.randint(key_count, (tile_total,), SLOTS // 8, SLOTS // 2 + 1)
    heavy = jax.random.randint(key_hot, (tile_total,), 0, 8) == 0
    chosen = jax.random.randint(key_pick, (), 0, tile_total)
    heavy = heavy | (jnp.arange(tile_total) == chosen)
    counts = jnp.where(heavy, SLOTS, counts)
    block_rows = jax.random.randint(key_rows, (tile_total, SLOTS), 0, ROWBLK)
    block_rows = jnp.where(jnp.arange(SLOTS)[None, :] < counts[:, None], block_rows, ROWBLK)
    block_rows = jnp.sort(block_rows, axis=1)
    bounds = jnp.arange(ROWBLK + 1)
    pointers = jnp.sum((block_rows[:, None, :] < bounds[None, :, None]).astype(jnp.int32), axis=2)
    return pointers.reshape(N_LOOP, N_WIDE, ROWBLK + 1).astype(jnp.int32)


def touch_ends(array, stream_key, smallest, high):
    longest = array.shape.index(max(array.shape))
    spots = []
    for shift in (0, 1):
        where = [jax.random.randint(jax.random.fold_in(stream_key, axis), (), 0, length) for axis, length in enumerate(array.shape)]
        where[longest] = (where[longest] + shift) % array.shape[longest]
        spots.append(tuple(where))
    return array.at[spots[0]].set(smallest).at[spots[1]].set(high)


def raised(entries, stream_key, source, target, parts, factor):
    owner, partner = [(jnp.arange(entries.shape[dim]) // (entries.shape[dim] // parts)).reshape([-1 if axis == dim else 1 for axis in range(entries.ndim)]) for dim in (source, target)]
    chosen = jax.random.permutation(stream_key, parts)[partner]
    strong = (owner == chosen) | (owner == (partner + parts // 2) % parts)
    return jnp.where(strong, factor * entries, entries)


def level_of(rng, shape, cuts, least, high):
    level, own = 1.0, jax.random.fold_in(rng, 6)
    for dim, parts in cuts:
        draws = jnp.exp(jax.random.uniform(jax.random.fold_in(own, dim), (parts,), jnp.float32, least / len(cuts), high / len(cuts)))
        level = level * jnp.repeat(draws, shape[dim] // parts).reshape([-1 if axis == dim else 1 for axis in range(len(shape))])
    return level


def bell_draw(key, extent, deviation, bound, shards=(), kind=jnp.bfloat16):
    array = jax.random.normal(key, extent, jnp.float32) * deviation
    if len(shards) > 0:
        array = level_of(key, extent, shards, -0.22, 0.18) * array
    return jnp.clip(array, min=-bound, max=bound).astype(kind)


def noise_with(stream_key, dims, width, limit, cuts, heavy, kind=jnp.bfloat16):
    drawn = width * jax.random.normal(stream_key, dims, jnp.float32)
    if cuts:
        drawn = drawn * level_of(stream_key, dims, cuts, -0.22, 0.18)
    return jnp.clip(raised(drawn, jax.random.fold_in(stream_key, 3), *heavy), -limit, limit).astype(kind)


def setup_inputs(seed: int = 0) -> dict:
    splits = jax.random.split(jax.random.key(seed), 8)
    return {
        "feats": noise_with(splits[0], (N_WIDE, ROWS_W, D), 1.0, 6.0, ((0, 16), (1, 8)), (0, 2, 16, 2.0)),
        "w_first": bell_draw(splits[1], (D, HID), D ** -0.5, 0.375),
        "w_second": bell_draw(splits[2], (HID, D), HID ** -0.5, 0.1875),
        "cotangent": bell_draw(splits[3], (N_WIDE, ROWS_W, D), ((ITEMS_DEV * N_LOOP * N_WIDE) ** -0.5), 0.078125, ((0, 16), (1, 8))),
        "block_values": bell_draw(splits[4], (N_LOOP, N_WIDE, SLOTS, BLK, BLK), (BLK * BPR) ** -0.5, 0.25, ((0, 8), (1, 16))),
        "row_ptr": draw_row_ptr(jax.random.fold_in(splits[7], 71), 0),
        "col_idx": touch_ends(jax.random.randint(splits[6], (N_LOOP, N_WIDE, SLOTS), 0, COLBLK), jax.random.fold_in(splits[6], 1), 0, COLBLK - 1).astype(jnp.int32),
    }


ALPHA = 0.1


def slot_layout(pointers, slot_total):
    slot_ids = jnp.arange(slot_total, dtype=jnp.int32)
    slot_row = jnp.sum((pointers[..., 1:, None] <= slot_ids).astype(jnp.int32), axis=-2)
    slot_live = (slot_ids < pointers[..., -1:]).astype(jnp.float32)
    return jnp.minimum(slot_row, pointers.shape[-1] - 2).astype(jnp.int32), slot_live


def silu_slope(value):
    sigma = jax.nn.sigmoid(value)
    return sigma * (1.0 + value * (1.0 - sigma))


def forward_step(current, teleport, tile_values, slot_row, slot_live, slot_col):
    col_major = current.reshape(N_WIDE, N_LOOP, ITEMS_DEV, D).transpose(1, 0, 2, 3).reshape(N_LOOP, COLBLK, BLK, D)

    def add_loop(summed, pieces):
        col_part, values_part, row_part, live_part, slot_part = pieces
        picked = col_part[slot_part].astype(jnp.float32)
        products = jnp.einsum("wsij,wsjd->wsid", values_part, picked) * live_part[:, :, None, None]
        landed = jax.vmap(lambda prod_one, row_one: jax.ops.segment_sum(prod_one, row_one, num_segments=ROWBLK))(products, row_part)
        return summed + landed, None

    start_sum = jnp.zeros((N_WIDE, ROWBLK, BLK, D), jnp.float32)
    summed, _ = lax.scan(add_loop, start_sum, (col_major, tile_values, slot_row, slot_live, slot_col))
    mixed = (1.0 - ALPHA) * summed.reshape(N_WIDE, ROWS_W, D) + ALPHA * teleport.astype(jnp.float32)
    return mixed.astype(jnp.bfloat16)


def adjoint_step(current, tile_values, slot_row, slot_live, slot_col):
    row_blocks = current.reshape(N_WIDE, ROWBLK, BLK, D)

    def one_loop(pieces):
        values_part, row_part, live_part, slot_part = pieces
        picked = jax.vmap(lambda block_rows, row_one: block_rows[row_one])(row_blocks, row_part).astype(jnp.float32)
        products = jnp.einsum("wsij,wsid->wsjd", values_part, picked) * live_part[:, :, None, None]
        landed = jax.ops.segment_sum(products.reshape(-1, BLK, D), slot_part.reshape(-1), num_segments=COLBLK)
        return landed.reshape(N_WIDE, ITEMS_DEV, D)

    spread = lax.map(one_loop, (tile_values, slot_row, slot_live, slot_col))
    moved = spread.transpose(1, 0, 2, 3).reshape(N_WIDE, ROWS_W, D)
    return ((1.0 - ALPHA) * moved).astype(jnp.bfloat16)


def reference(feats, w_first, w_second, cotangent, block_values, row_ptr, col_idx):
    slot_row, slot_live = slot_layout(row_ptr, SLOTS)
    tile_values = block_values.astype(jnp.float32)
    flat_feats = feats.reshape(ITEMS, D)
    pre_act = jnp.dot(flat_feats, w_first, preferred_element_type=jnp.float32)
    hidden = jax.nn.silu(pre_act).astype(jnp.bfloat16)
    teleport = jnp.dot(hidden, w_second, preferred_element_type=jnp.float32).astype(jnp.bfloat16)
    teleport = teleport.reshape(N_WIDE, ROWS_W, D)
    current = teleport
    for _ in range(STEPS):
        current = forward_step(current, teleport, tile_values, slot_row, slot_live, col_idx)
    adjoint_now = cotangent
    collected = cotangent.astype(jnp.float32)
    for repeat in range(STEPS):
        adjoint_now = adjoint_step(adjoint_now, tile_values, slot_row, slot_live, col_idx)
        if repeat < STEPS - 1:
            collected = collected + adjoint_now.astype(jnp.float32)
    grad_teleport = (ALPHA * collected + adjoint_now.astype(jnp.float32)).astype(jnp.bfloat16).reshape(ITEMS, D)
    grad_hidden = jnp.dot(grad_teleport, w_second.T, preferred_element_type=jnp.float32)
    grad_pre = (grad_hidden * silu_slope(pre_act)).astype(jnp.bfloat16)
    grad_first = jnp.dot(flat_feats.T, grad_pre, preferred_element_type=jnp.float32)
    grad_second = jnp.dot(hidden.T, grad_teleport, preferred_element_type=jnp.float32)
    return current, grad_first, grad_second
```

```python
import functools

import jax
import jax.numpy as jnp
import numpy as np
from jax import lax
from jax.experimental import pallas as pl
from jax.experimental.pallas import tpu as pltpu
from jax.sharding import Mesh
from jax.sharding import PartitionSpec as P

STEPS = 3
ALPHA = 0.1
AXES = ("zl", "y", "zh", "x", "c")
SIZES = (2, 4, 2, 4, 2)
LOOP = ("zl", "y")
WIDE = ("zh", "x", "c")
BLK = 64
DIM = 256
ITEMS = 256
PIECE = 2 * ITEMS
PAIR = 2 * PIECE
GRAPH = 4 * PAIR
SLOTS = 80
HALF = SLOTS // 2


def permutation(move):
    pairs = []
    for source in range(int(np.prod(SIZES))):
        place = dict(zip(AXES, np.unravel_index(source, SIZES)))
        place = {name: int(value) for name, value in place.items()}
        place.update(move(place))
        pairs.append((source, int(np.ravel_multi_index([place[name] for name in AXES], SIZES))))
    return pairs


def send(value, move):
    return lax.ppermute(value, AXES, permutation(move))


def core_move(place):
    return {"c": 1 - place["c"]}


def gather_z(place):
    return {"zl": 1 - place["zl"]} if place["c"] else {"zh": 1 - place["zh"]}


def scatter_z(place):
    return {"zh": 1 - place["zh"]} if place["c"] else {"zl": 1 - place["zl"]}


def gather_ring(step, place):
    return {"y": (place["y"] + step) % 4} if place["c"] else {"x": (place["x"] + step) % 4}


def scatter_ring(step, place):
    return {"x": (place["x"] + step) % 4} if place["c"] else {"y": (place["y"] + step) % 4}


def product_kernel(meta, values, part0, part1, part2, part3, out0, out1, out2, out3, gathered, sums, sems):
    copies = [
        pltpu.make_async_copy(part, gathered.at[pl.ds(index * PAIR, PAIR)], sems.at[index])
        for index, part in enumerate((part0, part1, part2, part3))
    ]
    for copy in copies:
        copy.start()
    sums[...] = jnp.zeros_like(sums)
    for copy in copies:
        copy.wait()

    def run(tile, half):
        live = meta[2, tile * SLOTS]
        count = jnp.clip(live - half * HALF, 0, HALF)

        def four(group, carry):
            products = []
            for lane in range(4):
                slot = group * 4 + lane
                source = pl.multiple_of(meta[0, tile * SLOTS + half * HALF + slot], BLK)
                block = values[tile * HALF + slot][:, half * BLK : (half + 1) * BLK]
                products.append(
                    jnp.dot(block, gathered[pl.ds(source, BLK), :], preferred_element_type=jnp.float32)
                )
            for lane in range(4):
                target = pl.multiple_of(meta[1, tile * SLOTS + half * HALF + group * 4 + lane], BLK)
                sums[pl.ds(target, BLK), :] += products[lane]
            return carry

        lax.fori_loop(0, (count + 3) // 4, four, 0)

    for tile in range(2):
        for half in range(2):
            run(tile, half)
    for index, out in enumerate((out0, out1, out2, out3)):
        out[...] = sums[index * PAIR : (index + 1) * PAIR, :].astype(out.dtype)


def block_product(meta, values, parts):
    piece = jax.ShapeDtypeStruct((PAIR, DIM), jnp.bfloat16)
    return pl.pallas_call(
        product_kernel,
        out_shape=(piece,) * 4,
        in_specs=[
            pl.BlockSpec(memory_space=pltpu.SMEM),
            pl.BlockSpec(memory_space=pltpu.VMEM),
        ]
        + [pl.BlockSpec(memory_space=pl.ANY)] * 4,
        out_specs=(pl.BlockSpec(memory_space=pltpu.VMEM),) * 4,
        scratch_shapes=[
            pltpu.VMEM((GRAPH, DIM), jnp.bfloat16),
            pltpu.VMEM((GRAPH + BLK, DIM), jnp.float32),
            pltpu.SemaphoreType.DMA((4,)),
        ],
        compiler_params=pltpu.CompilerParams(vmem_limit_bytes=40 * 2**20),
        name="block_product",
    )(meta, values, *parts)


def slot_tables(pointers, columns, zl, y, zh, x, core):
    slot_ids = jnp.arange(SLOTS, dtype=jnp.int32)
    rows = jnp.sum((pointers[:, 1:, None] <= slot_ids).astype(jnp.int32), axis=1)
    rows = jnp.minimum(rows, pointers.shape[1] - 2)
    live_count = pointers[:, -1:]
    live = slot_ids[None, :] < live_count
    tile = jnp.arange(2, dtype=jnp.int32)[:, None]
    row_l = rows // 4
    row_zl, row_y = row_l // 4, row_l % 4
    row_base = (row_zl ^ zl) * PIECE + tile * ITEMS + (rows % 4) * BLK
    col_w = columns // 4
    col_zh, col_x, col_c = col_w // 8, (col_w // 2) % 4, col_w % 2
    col_base = (col_zh ^ zh) * PIECE + col_c * ITEMS + (columns % 4) * BLK
    forward_source = ((x - col_x) % 4) * PAIR + col_base
    forward_target = ((row_y - y) % 4) * PAIR + row_base
    adjoint_source = ((y - row_y) % 4) * PAIR + row_base
    adjoint_target = ((col_x - x) % 4) * PAIR + col_base
    source = jnp.where(core == 0, forward_source, adjoint_source)
    target = jnp.where(core == 0, forward_target, adjoint_target)
    source = jnp.where(live, source, 0)
    target = jnp.where(live, target, GRAPH)
    counts = jnp.broadcast_to(live_count, source.shape)
    return jnp.stack([source, target, counts]).reshape(3, 2 * SLOTS)


def silu_slope(value):
    sigma = jax.nn.sigmoid(value)
    return sigma * (1.0 + value * (1.0 - sigma))


def by_tile(own, other, core):
    return jnp.where(core == 0, jnp.stack([own, other]), jnp.stack([other, own]))


def body(feats, w_first, w_second, cotangent, block_values, row_ptr, col_idx):
    f32, bf16 = jnp.float32, jnp.bfloat16
    zl, y, zh, x, core = (lax.axis_index(name) for name in AXES)
    own_feats, own_cot = feats[0], cotangent[0]
    other = send(jnp.concatenate([own_feats, own_cot]), core_move)
    tile = block_values[0, 0]
    packed = jnp.concatenate([tile[:HALF], tile[HALF:]], axis=-1)
    other_packed = send(packed, core_move)
    table = jnp.concatenate([row_ptr[0, 0], col_idx[0, 0]])
    other_table = send(table, core_move)

    chip_feats = by_tile(own_feats, other[:ITEMS], core).reshape(PIECE, DIM)
    chip_cot = by_tile(own_cot, other[ITEMS:], core).reshape(PIECE, DIM)
    pre_act = jnp.dot(chip_feats, w_first, preferred_element_type=f32)
    hidden = jax.nn.silu(pre_act).astype(bf16)
    teleport = jnp.dot(hidden, w_second, preferred_element_type=f32).astype(bf16)

    tables = by_tile(table, other_table, core)
    meta = slot_tables(tables[:, :33], tables[:, 33:], zl, y, zh, x, core)
    values = by_tile(packed, other_packed, core)
    flipped = jnp.concatenate(
        [jnp.swapaxes(values[..., :BLK], -1, -2), jnp.swapaxes(values[..., BLK:], -1, -2)], axis=-1
    )
    values = jnp.where(core == 0, values, flipped).reshape(2 * HALF, BLK, 2 * BLK)

    state = jnp.where(core == 0, teleport, chip_cot)
    restart = jnp.where(core == 0, ALPHA, 0.0).astype(f32)
    collected = state.astype(f32)
    for step in range(STEPS):
        z_piece = send(state, gather_z)
        pair = jnp.concatenate([state, z_piece])
        parts = [pair] + [send(pair, functools.partial(gather_ring, hop)) for hop in (1, 2, 3)]
        outs = block_product(meta, values, parts)
        got = [outs[0]] + [send(outs[hop], functools.partial(scatter_ring, hop)) for hop in (1, 2, 3)]
        far = sum(piece[PIECE:].astype(f32) for piece in got).astype(bf16)
        back = send(far, scatter_z)
        summed = sum(piece[:PIECE].astype(f32) for piece in got) + back.astype(f32)
        state = ((1.0 - ALPHA) * summed + restart * teleport.astype(f32)).astype(bf16)
        if step < STEPS - 1:
            collected = collected + state.astype(f32)
    grad_own = (ALPHA * collected + state.astype(f32)).astype(bf16)
    ending = send(jnp.where(core == 0, state, grad_own), core_move)
    propagated = jnp.where(core == 0, state[:ITEMS], ending[ITEMS:])
    grad_teleport = jnp.where(core == 0, ending, grad_own)

    grad_hidden = lax.dot_general(
        grad_teleport, w_second, (((1,), (1,)), ((), ())), preferred_element_type=f32
    )
    grad_pre = (grad_hidden * silu_slope(pre_act)).astype(bf16)
    contract_items = (((0,), (0,)), ((), ()))
    feats_part = lax.dynamic_index_in_dim(chip_feats.reshape(PIECE, 8, 2, 16), core, 2, False).reshape(PIECE, 128)
    hidden_part = lax.dynamic_index_in_dim(hidden.reshape(PIECE, 8, 2, 64), core, 2, False).reshape(PIECE, 512)
    first = lax.dot_general(feats_part, grad_pre, contract_items, preferred_element_type=f32).astype(bf16)
    second = lax.dot_general(hidden_part, grad_teleport, contract_items, preferred_element_type=f32).astype(bf16)
    first = first.reshape(8, 16, 8, 128).transpose(2, 0, 1, 3)
    second = second.reshape(8, 4, 16, 2, 128).transpose(3, 1, 0, 2, 4).reshape(8, 8, 16, 128)
    spread = jnp.concatenate([first, second], axis=2).reshape(64, 32, 128)
    landed = lax.all_to_all(spread, ("zl", "y", "zh", "x"), 0, 0)
    mine = jnp.sum(landed.astype(f32), axis=0)
    z_mine = send(mine, lambda place: {"zl": 1 - place["zl"]})
    both = jnp.where(zl == 0, jnp.stack([mine, z_mine]), jnp.stack([z_mine, mine]))
    ring = [both] + [
        send(both, functools.partial(lambda hop, place: {"y": (place["y"] + hop) % 4}, hop)) for hop in (1, 2, 3)
    ]
    ring = jnp.stack(ring)
    order = (y - jnp.arange(4)) % 4
    ring = ring[order].transpose(1, 0, 2, 3).reshape(8, 32, 128)
    grad_first = ring[:, :16].transpose(1, 0, 2).reshape(16, 1024)
    grad_second = ring[:, 16:].reshape(2, 4, 16, 128).transpose(1, 2, 0, 3).reshape(64, 256)
    return (propagated[None], grad_first, grad_second)


def solution(mesh):
    fine = Mesh(mesh.devices.reshape(SIZES), AXES)
    return jax.shard_map(
        body,
        mesh=fine,
        in_specs=(
            P(WIDE, LOOP, None),
            P(),
            P(),
            P(WIDE, LOOP, None),
            P(LOOP, WIDE, None, None, None),
            P(LOOP, WIDE, None),
            P(LOOP, WIDE, None),
        ),
        out_specs=(P(WIDE, LOOP, None), P(WIDE, None), P(WIDE, None)),
        check_vma=False,
    )
```

```python
import functools

import jax
import jax.numpy as jnp
import numpy as np
from jax import lax
from jax.experimental import pallas as pl
from jax.experimental.pallas import tpu as pltpu
from jax.sharding import Mesh
from jax.sharding import PartitionSpec as P

STEPS = 3
ALPHA = 0.1
AXES = ("zl", "y", "zh", "x", "c")
SIZES = (2, 4, 2, 4, 2)
LOOP = ("zl", "y")
WIDE = ("zh", "x", "c")
BLK = 64
DIM = 256
ITEMS = 256
PIECE = 2 * ITEMS
SLOTS = 80
PACK = 32
LANES = 128
STATE = 1024
GRAPH = 4 * STATE
TILES = 8
GROUP = 8


def permutation(move):
    pairs = []
    for source in range(int(np.prod(SIZES))):
        place = dict(zip(AXES, np.unravel_index(source, SIZES)))
        place = {name: int(value) for name, value in place.items()}
        place.update(move(place))
        pairs.append((source, int(np.ravel_multi_index([place[name] for name in AXES], SIZES))))
    return pairs


def send(value, move):
    return lax.ppermute(value, AXES, permutation(move))


def core_move(place):
    return {"c": 1 - place["c"]}


def z_move(step, place):
    spot = (2 * place["zh"] + place["zl"] + step) % 4
    return {"zh": spot // 2, "zl": spot % 2}


def gather_ring(step, place):
    return {"y": (place["y"] + step) % 4} if place["c"] else {"x": (place["x"] + step) % 4}


def scatter_ring(step, place):
    return {"x": (place["x"] + step) % 4} if place["c"] else {"y": (place["y"] + step) % 4}


def product_kernel(meta, masks, *refs):
    tiles, parts, outs = refs[:TILES], refs[TILES : TILES + 4], refs[TILES + 4 : TILES + 8]
    values, gathered, sums, sems = refs[TILES + 8 :]
    copies = [
        pltpu.make_async_copy(part, gathered.at[pl.ds(index * STATE, STATE)], sems.at[TILES + index])
        for index, part in enumerate(parts)
    ]
    copies += [
        pltpu.make_async_copy(tile.at[pl.ds(0, SLOTS)], values.at[pl.ds(index * SLOTS, SLOTS)], sems.at[index])
        for index, tile in enumerate(tiles)
    ]
    for copy in copies:
        copy.start()
    sums[...] = jnp.zeros_like(sums)
    for copy in copies:
        copy.wait()
    adjoint = meta[2, TILES]
    left, right = masks[0], masks[1]

    def one_tile(tile, carry):
        first = tile * SLOTS
        live = meta[2, tile]

        def group(index, inner):
            products = []
            for lane in range(GROUP):
                slot = first + index * GROUP + lane
                entries = values[slot]
                source = pl.multiple_of(meta[0, slot], PACK)
                vectors = gathered[pl.ds(source, PACK), :]
                rows = jnp.where(adjoint == 0, entries, vectors)
                cols = jnp.where(adjoint == 0, vectors, entries)
                turned = pltpu.roll(cols, BLK, 1)
                spread = jnp.concatenate([cols * left, turned * left, turned * right, cols * right], axis=0)
                products.append(jnp.dot(rows, spread, preferred_element_type=jnp.float32))
            for lane in range(GROUP):
                target = pl.multiple_of(meta[1, first + index * GROUP + lane], PACK)
                sums[pl.ds(target, PACK), :] += products[lane]
            return inner

        return lax.fori_loop(0, (live + GROUP - 1) // GROUP, group, carry)

    lax.fori_loop(0, TILES, one_tile, 0)
    for index, out in enumerate(outs):
        out[...] = sums[index * STATE : (index + 1) * STATE, :].astype(out.dtype)


def block_product(meta, masks, tiles, parts):
    piece = jax.ShapeDtypeStruct((STATE, LANES), jnp.bfloat16)
    return pl.pallas_call(
        product_kernel,
        out_shape=(piece,) * 4,
        in_specs=[
            pl.BlockSpec(memory_space=pltpu.SMEM),
            pl.BlockSpec(memory_space=pltpu.VMEM),
        ]
        + [pl.BlockSpec(memory_space=pl.ANY)] * (TILES + 4),
        out_specs=(pl.BlockSpec(memory_space=pltpu.VMEM),) * 4,
        scratch_shapes=[
            pltpu.VMEM((TILES * SLOTS, PACK, LANES), jnp.bfloat16),
            pltpu.VMEM((GRAPH, LANES), jnp.bfloat16),
            pltpu.VMEM((GRAPH + PACK, LANES), jnp.float32),
            pltpu.SemaphoreType.DMA((TILES + 4,)),
        ],
        compiler_params=pltpu.CompilerParams(vmem_limit_bytes=40 * 2**20),
        name="block_product",
    )(meta, masks, *tiles, *parts)


def slot_tables(pointers, columns, zl, y, zh, x, core):
    slot_ids = jnp.arange(SLOTS, dtype=jnp.int32)
    rows = jnp.sum((pointers[:, 1:, None] <= slot_ids).astype(jnp.int32), axis=1)
    rows = jnp.minimum(rows, pointers.shape[1] - 2)
    live_count = pointers[:, -1]
    live = slot_ids[None, :] < live_count[:, None]
    place = jnp.arange(TILES, dtype=jnp.int32)
    spot = 2 * zh + zl
    from_z = (spot - place // 2) % 4
    tile_zh, tile_zl = (from_z // 2)[:, None], (from_z % 2)[:, None]
    tile_core = (core ^ (place % 2))[:, None]
    row_l = rows // 4
    row_y, row_z = row_l % 4, 2 * tile_zh + row_l // 4
    row_base = ((spot - row_z) % 4) * 8 + tile_core * 4 + rows % 4
    col_w = columns // 4
    col_x, col_z = (col_w // 2) % 4, 2 * (col_w // 8) + tile_zl
    col_base = ((spot - col_z) % 4) * 8 + (col_w % 2) * 4 + columns % 4
    forward_source = ((x - col_x) % 4) * STATE + col_base * PACK
    forward_target = ((row_y - y) % 4) * STATE + row_base * PACK
    adjoint_source = ((y - row_y) % 4) * STATE + row_base * PACK
    adjoint_target = ((col_x - x) % 4) * STATE + col_base * PACK
    source = jnp.where(live, jnp.where(core == 0, forward_source, adjoint_source), 0)
    target = jnp.where(live, jnp.where(core == 0, forward_target, adjoint_target), GRAPH)
    counts = jnp.concatenate([live_count, core[None], jnp.zeros((TILES * SLOTS - TILES - 1,), jnp.int32)])
    return jnp.stack([source.reshape(-1), target.reshape(-1), counts])


def pack_rows(blocks):
    return jnp.concatenate([blocks[..., :PACK, :], blocks[..., PACK:, :]], axis=-1)


def unpack_rows(blocks):
    return jnp.concatenate([blocks[..., :BLK], blocks[..., BLK:]], axis=-2)


def split_features(chip_state, core):
    blocks = chip_state.reshape(8, BLK, 4, BLK).transpose(2, 0, 1, 3)
    blocks = jnp.where(core == 0, blocks, jnp.swapaxes(blocks, -1, -2))
    return pack_rows(blocks).reshape(4, 8 * PACK, LANES)


def join_features(pieces, core):
    blocks = unpack_rows(pieces.reshape(4, 8, PACK, LANES))
    blocks = jnp.where(core == 0, blocks, jnp.swapaxes(blocks, -1, -2))
    return blocks.transpose(1, 2, 0, 3).reshape(PIECE, DIM)


def silu_slope(value):
    sigma = jax.nn.sigmoid(value)
    return sigma * (1.0 + value * (1.0 - sigma))


def by_tile(own, other, core):
    return jnp.where(core == 0, jnp.stack([own, other]), jnp.stack([other, own]))


def body(feats, w_first, w_second, cotangent, block_values, row_ptr, col_idx):
    f32, bf16 = jnp.float32, jnp.bfloat16
    zl, y, zh, x, core = (lax.axis_index(name) for name in AXES)
    spot = 2 * zh + zl
    table = jnp.zeros((1, PACK, LANES), bf16)
    table = table.at[0, 0, :33].set(row_ptr[0, 0].astype(bf16)).at[0, 1, :SLOTS].set(col_idx[0, 0].astype(bf16))
    tile = jnp.concatenate([pack_rows(block_values[0, 0]), table])
    same_core = [tile] + [send(tile, functools.partial(z_move, hop)) for hop in (1, 2, 3)]
    tiles = []
    for mine in same_core:
        tiles += [mine, send(mine, core_move)]

    own_feats, own_cot = feats[0], cotangent[0]
    other = send(jnp.concatenate([own_feats, own_cot]), core_move)
    chip_feats = by_tile(own_feats, other[:ITEMS], core).reshape(PIECE, DIM)
    chip_cot = by_tile(own_cot, other[ITEMS:], core).reshape(PIECE, DIM)
    pre_act = jnp.dot(chip_feats, w_first, preferred_element_type=f32)
    hidden = jax.nn.silu(pre_act).astype(bf16)
    teleport = jnp.dot(hidden, w_second, preferred_element_type=f32).astype(bf16)

    tables = jnp.stack([piece[SLOTS] for piece in tiles])
    meta = slot_tables(
        tables[:, 0, :33].astype(jnp.int32), tables[:, 1, :SLOTS].astype(jnp.int32), zl, y, zh, x, core
    )
    lanes = jnp.arange(LANES)
    masks = jnp.stack([lanes < BLK, lanes >= BLK]).astype(bf16)
    masks = jnp.broadcast_to(masks[:, None, :], (2, PACK, LANES))

    start = split_features(jnp.where(core == 0, teleport, chip_cot), core)
    start = [lax.dynamic_index_in_dim(start, (spot + hop) % 4, 0, False) for hop in range(4)]
    state = jnp.concatenate(
        [start[0]] + [send(start[hop], functools.partial(z_move, hop)) for hop in (1, 2, 3)]
    )
    restart = jnp.where(core == 0, ALPHA, 0.0).astype(f32)
    constant = restart * state.astype(f32)
    collected = state.astype(f32)
    for step in range(STEPS):
        parts = [state] + [send(state, functools.partial(gather_ring, hop)) for hop in (1, 2, 3)]
        outs = block_product(meta, masks, tiles, parts)
        got = [outs[0]] + [send(outs[hop], functools.partial(scatter_ring, hop)) for hop in (1, 2, 3)]
        summed = sum(piece.astype(f32) for piece in got)
        state = ((1.0 - ALPHA) * summed + constant).astype(bf16)
        if step < STEPS - 1:
            collected = collected + state.astype(f32)
    last = jnp.where(core == 0, state, (ALPHA * collected + state.astype(f32)).astype(bf16))
    last = last.reshape(4, 8 * PACK, LANES)
    pieces = [last[0]] + [send(last[hop], functools.partial(z_move, -hop)) for hop in (1, 2, 3)]
    pieces = jnp.stack(pieces)[(jnp.arange(4) - spot) % 4]
    joined = join_features(pieces, core)
    ending = send(joined, core_move)
    propagated = jnp.where(core == 0, joined[:ITEMS], ending[ITEMS:])
    grad_teleport = jnp.where(core == 0, ending, joined)

    grad_hidden = lax.dot_general(
        grad_teleport, w_second, (((1,), (1,)), ((), ())), preferred_element_type=f32
    )
    grad_pre = (grad_hidden * silu_slope(pre_act)).astype(bf16)
    contract_items = (((0,), (0,)), ((), ()))
    feats_part = lax.dynamic_index_in_dim(chip_feats.reshape(PIECE, 8, 2, 16), core, 2, False).reshape(PIECE, 128)
    hidden_part = lax.dynamic_index_in_dim(hidden.reshape(PIECE, 8, 2, 64), core, 2, False).reshape(PIECE, 512)
    first = lax.dot_general(feats_part, grad_pre, contract_items, preferred_element_type=f32).astype(bf16)
    second = lax.dot_general(hidden_part, grad_teleport, contract_items, preferred_element_type=f32).astype(bf16)
    first = first.reshape(8, 16, 8, 128).transpose(2, 0, 1, 3)
    second = second.reshape(8, 4, 16, 2, 128).transpose(3, 1, 0, 2, 4).reshape(8, 8, 16, 128)
    spread = jnp.concatenate([first, second], axis=2).reshape(64, 32, 128)
    landed = lax.all_to_all(spread, ("zl", "y", "zh", "x"), 0, 0)
    mine = jnp.sum(landed.astype(f32), axis=0)
    z_mine = send(mine, lambda place: {"zl": 1 - place["zl"]})
    both = jnp.where(zl == 0, jnp.stack([mine, z_mine]), jnp.stack([z_mine, mine]))
    ring = [both] + [
        send(both, functools.partial(lambda hop, place: {"y": (place["y"] + hop) % 4}, hop)) for hop in (1, 2, 3)
    ]
    ring = jnp.stack(ring)
    order = (y - jnp.arange(4)) % 4
    ring = ring[order].transpose(1, 0, 2, 3).reshape(8, 32, 128)
    grad_first = ring[:, :16].transpose(1, 0, 2).reshape(16, 1024)
    grad_second = ring[:, 16:].reshape(2, 4, 16, 128).transpose(1, 2, 0, 3).reshape(64, 256)
    return (propagated[None], grad_first, grad_second)


def solution(mesh):
    fine = Mesh(mesh.devices.reshape(SIZES), AXES)
    return jax.shard_map(
        body,
        mesh=fine,
        in_specs=(
            P(WIDE, LOOP, None),
            P(),
            P(),
            P(WIDE, LOOP, None),
            P(LOOP, WIDE, None, None, None),
            P(LOOP, WIDE, None),
            P(LOOP, WIDE, None),
        ),
        out_specs=(P(WIDE, LOOP, None), P(WIDE, None), P(WIDE, None)),
        check_vma=False,
    )
```

```python
import functools

import jax
import jax.numpy as jnp
import numpy as np
from jax import lax
from jax.experimental import pallas as pl
from jax.experimental.pallas import tpu as pltpu
from jax.sharding import Mesh
from jax.sharding import PartitionSpec as P

STEPS = 3
ALPHA = 0.1
AXES = ("zl", "y", "zh", "x", "c")
SIZES = (2, 4, 2, 4, 2)
LOOP = ("zl", "y")
WIDE = ("zh", "x", "c")
BLK = 64
DIM = 256
ITEMS = 256
PIECE = 2 * ITEMS
SLOTS = 80
PACK = 32
LANES = 128
STATE = 1024
GRAPH = 4 * STATE
TILES = 8
GROUP = 32
LIST = TILES * SLOTS + 2 * GROUP


def permutation(move):
    pairs = []
    for source in range(int(np.prod(SIZES))):
        place = dict(zip(AXES, np.unravel_index(source, SIZES)))
        place = {name: int(value) for name, value in place.items()}
        place.update(move(place))
        pairs.append((source, int(np.ravel_multi_index([place[name] for name in AXES], SIZES))))
    return pairs


def send(value, move):
    return lax.ppermute(value, AXES, permutation(move))


def core_move(place):
    return {"c": 1 - place["c"]}


def z_move(step, place):
    spot = (2 * place["zh"] + place["zl"] + step) % 4
    return {"zh": spot // 2, "zl": spot % 2}


def relay_move(place):
    return z_move(3 if place["c"] else 1, place)


def gather_ring(step, place):
    return {"y": (place["y"] + step) % 4} if place["c"] else {"x": (place["x"] + step) % 4}


def scatter_ring(step, place):
    return {"x": (place["x"] + step) % 4} if place["c"] else {"y": (place["y"] + step) % 4}


def start_kernel(place, own, other, w_first, w_second, out):
    core, spot = place[0], place[1]
    for tile in range(2):
        rows = jnp.where(core == tile, own[...], other[...])
        pre_act = jnp.dot(rows[:ITEMS], w_first[...], preferred_element_type=jnp.float32)
        hidden = (pre_act / (1.0 + jnp.exp(-pre_act))).astype(jnp.bfloat16)
        teleport = jnp.dot(hidden, w_second[...], preferred_element_type=jnp.float32)
        straight = jnp.where(core == 0, teleport, rows[ITEMS:PIECE].astype(jnp.float32).T)
        for corner in range(4):
            pieces = []
            for block in range(4):
                low, high = block * BLK, corner * BLK
                first = jnp.where(core == 0, straight[low : low + BLK, high : high + BLK], straight[high : high + BLK, low : low + BLK])
                pieces.append(jnp.concatenate([first[:PACK], first[PACK:]], axis=1))
            spread = jnp.concatenate(pieces, axis=0).astype(jnp.bfloat16)
            out[(corner - spot) % 4, tile * ITEMS // 2 : (tile + 1) * ITEMS // 2, :] = spread
    for hop in range(4):
        out[hop, ITEMS : ITEMS + 16, :] = own[PIECE:, :LANES]
        out[hop, ITEMS + 16 :, :] = other[PIECE:, :LANES]


def start_pieces(place, own, other, w_first, w_second):
    return pl.pallas_call(
        start_kernel,
        out_shape=jax.ShapeDtypeStruct((4, 9 * PACK, LANES), jnp.bfloat16),
        in_specs=[pl.BlockSpec(memory_space=pltpu.SMEM)] + [pl.BlockSpec(memory_space=pltpu.VMEM)] * 4,
        out_specs=pl.BlockSpec(memory_space=pltpu.VMEM),
        compiler_params=pltpu.CompilerParams(vmem_limit_bytes=24 * 2**20),
        name="start_pieces",
    )(place, own, other, w_first, w_second)


def product_kernel(meta, masks, *refs):
    tiles, parts, outs = refs[:TILES], refs[TILES : TILES + 4], refs[TILES + 4 : TILES + 8]
    values, gathered, sums, sems = refs[TILES + 8 :]
    part_copies = [
        pltpu.make_async_copy(part, gathered.at[pl.ds(index * STATE, STATE)], sems.at[TILES + index])
        for index, part in enumerate(parts)
    ]
    tile_copies = [
        pltpu.make_async_copy(tile, values.at[pl.ds(index * SLOTS * PACK, SLOTS * PACK)], sems.at[index])
        for index, tile in enumerate(tiles)
    ]
    for copy in tile_copies[: TILES // 2] + part_copies + tile_copies[TILES // 2 :]:
        copy.start()
    sums[...] = jnp.zeros_like(sums)
    adjoint = meta[3, 2]
    left, right = masks[0], masks[1]

    def group(index, carry):
        first = index * GROUP
        products = []
        for lane in range(GROUP):
            entries = values[pl.ds(pl.multiple_of(meta[2, first + lane], PACK), PACK), :]
            source = pl.multiple_of(meta[0, first + lane], PACK)
            vectors = gathered[pl.ds(source, PACK), :]
            rows = jnp.where(adjoint == 0, entries, vectors)
            cols = jnp.where(adjoint == 0, vectors, entries)
            turned = pltpu.roll(cols, BLK, 1)
            spread = jnp.concatenate([cols * left, turned * left, turned * right, cols * right], axis=0)
            products.append(jnp.dot(rows, spread, preferred_element_type=jnp.float32))
        for lane in range(GROUP):
            target = pl.multiple_of(meta[1, first + lane], PACK)
            sums[pl.ds(target, PACK), :] += products[lane]
        return carry

    early = meta[3, 0] // GROUP
    total = (meta[3, 1] + GROUP - 1) // GROUP
    for copy in tile_copies[: TILES // 2] + part_copies:
        copy.wait()
    lax.fori_loop(0, early, group, 0)
    for copy in tile_copies[TILES // 2 :]:
        copy.wait()
    lax.fori_loop(early, total, group, 0)
    for index, out in enumerate(outs):
        out[...] = sums[index * STATE : (index + 1) * STATE, :].astype(out.dtype)


def block_product(meta, masks, tiles, parts):
    piece = jax.ShapeDtypeStruct((STATE, LANES), jnp.bfloat16)
    return pl.pallas_call(
        product_kernel,
        out_shape=(piece,) * 4,
        in_specs=[
            pl.BlockSpec(memory_space=pltpu.SMEM),
            pl.BlockSpec(memory_space=pltpu.VMEM),
        ]
        + [pl.BlockSpec(memory_space=pltpu.HBM)] * TILES
        + [pl.BlockSpec(memory_space=pl.ANY)] * 4,
        out_specs=(pl.BlockSpec(memory_space=pltpu.VMEM),) * 4,
        scratch_shapes=[
            pltpu.VMEM((TILES * SLOTS * PACK, LANES), jnp.bfloat16),
            pltpu.VMEM((GRAPH, LANES), jnp.bfloat16),
            pltpu.VMEM((GRAPH + PACK, LANES), jnp.float32),
            pltpu.SemaphoreType.DMA((TILES + 4,)),
        ],
        compiler_params=pltpu.CompilerParams(vmem_limit_bytes=20 * 2**20),
        name="block_product",
    )(meta, masks, *tiles, *parts)


def slot_tables(pointers, columns, zl, y, zh, x, core):
    slot_ids = jnp.arange(SLOTS, dtype=jnp.int32)
    rows = jnp.sum((pointers[:, 1:, None] <= slot_ids).astype(jnp.int32), axis=1)
    rows = jnp.minimum(rows, pointers.shape[1] - 2)
    live_count = pointers[:, -1]
    place = jnp.arange(TILES, dtype=jnp.int32)
    spot = 2 * zh + zl
    from_z = (spot - place) % 4
    tile_zh, tile_zl = (from_z // 2)[:, None], (from_z % 2)[:, None]
    tile_core = (core ^ (place // 4))[:, None]
    row_l = rows // 4
    row_y, row_z = row_l % 4, 2 * tile_zh + row_l // 4
    row_base = ((spot - row_z) % 4) * 8 + tile_core * 4 + rows % 4
    col_w = columns // 4
    col_x, col_z = (col_w // 2) % 4, 2 * (col_w // 8) + tile_zl
    col_base = ((spot - col_z) % 4) * 8 + (col_w % 2) * 4 + columns % 4
    forward_source = ((x - col_x) % 4) * STATE + col_base * PACK
    forward_target = ((row_y - y) % 4) * STATE + row_base * PACK
    adjoint_source = ((y - row_y) % 4) * STATE + row_base * PACK
    adjoint_target = ((col_x - x) % 4) * STATE + col_base * PACK
    source = jnp.where(core == 0, forward_source, adjoint_source)
    target = jnp.where(core == 0, forward_target, adjoint_target)
    codes = (source * (2 * GRAPH) + target).reshape(-1, 1)
    ends = jnp.cumsum(live_count)
    spots = jnp.arange(LIST, dtype=jnp.int32)
    passed = (spots[None, :] >= ends[:, None]).astype(jnp.int32)
    begin = jnp.sum(passed * live_count[:, None], axis=0)
    entry = jnp.minimum(jnp.sum(passed, axis=0), TILES - 1) * SLOTS + spots - begin
    hits = entry[None, :] == jnp.arange(TILES * SLOTS, dtype=jnp.int32)[:, None]
    codes = jnp.sum(jnp.where(hits, codes, 0), axis=0)
    listed = spots < ends[-1]
    source = jnp.where(listed, codes // (2 * GRAPH), 0)
    target = jnp.where(listed, codes % (2 * GRAPH), GRAPH)
    entry = jnp.where(listed, entry * PACK, 0)
    counts = jnp.where(spots == 0, ends[TILES // 2 - 1], jnp.where(spots == 1, ends[-1], core))
    return jnp.stack([source, target, entry, counts])


def pack_rows(blocks):
    return jnp.concatenate([blocks[..., :PACK, :], blocks[..., PACK:, :]], axis=-1)


def unpack_rows(blocks):
    return jnp.concatenate([blocks[..., :BLK], blocks[..., BLK:]], axis=-2)


def join_features(pieces, core):
    blocks = unpack_rows(pieces.reshape(4, 8, PACK, LANES))
    blocks = jnp.where(core == 0, blocks, jnp.swapaxes(blocks, -1, -2))
    return blocks.transpose(1, 2, 0, 3).reshape(PIECE, DIM)


def silu_slope(value):
    sigma = jax.nn.sigmoid(value)
    return sigma * (1.0 + value * (1.0 - sigma))


def by_tile(own, other, core):
    return jnp.where(core == 0, jnp.stack([own, other]), jnp.stack([other, own]))


def body(feats, w_first, w_second, cotangent, block_values, row_ptr, col_idx):
    f32, bf16 = jnp.float32, jnp.bfloat16
    zl, y, zh, x, core = (lax.axis_index(name) for name in AXES)
    spot = 2 * zh + zl
    table = jnp.concatenate([row_ptr[0, 0], col_idx[0, 0]]).astype(bf16)
    table = jnp.pad(table[None], ((0, 15), (0, DIM - 113)))
    message = jnp.concatenate([feats[0], cotangent[0], table])
    other = send(message, core_move)
    lanes = jnp.arange(LANES)
    masks = jnp.stack([lanes < BLK, lanes >= BLK]).astype(bf16)
    masks = jnp.broadcast_to(masks[:, None, :], (2, PACK, LANES))

    start = start_pieces(jnp.stack([core, spot]), message, other, w_first, w_second)
    tile = pack_rows(block_values[0, 0]).reshape(SLOTS * PACK, LANES)
    own_swapped = send(tile, core_move)
    start, own_swapped = lax.optimization_barrier((start, own_swapped))
    start = [start[0]] + [send(start[hop], functools.partial(z_move, hop)) for hop in (1, 2, 3)]
    ahead = send(tile, functools.partial(z_move, 1))
    behind = send(tile, functools.partial(z_move, 3))
    start, ahead, behind = lax.optimization_barrier((start, ahead, behind))
    across = send(jnp.where(core == 0, ahead, behind), relay_move)
    state = jnp.concatenate([piece[:ITEMS] for piece in start])
    tables = jnp.stack([piece[ITEMS : ITEMS + PACK : 16] for piece in start]).astype(jnp.int32)
    tables = tables.transpose(1, 0, 2).reshape(TILES, LANES)
    meta = slot_tables(tables[:, :33], tables[:, 33:113], zl, y, zh, x, core)
    first_parts = [state] + [send(state, functools.partial(gather_ring, hop)) for hop in (1, 2, 3)]
    first_parts, across, meta = lax.optimization_barrier((first_parts, across, meta))
    same_core = [tile, ahead, across, behind]
    tiles = same_core + [own_swapped] + [send(piece, core_move) for piece in same_core[1:]]

    chip_feats = by_tile(message[:ITEMS], other[:ITEMS], core).reshape(PIECE, DIM)
    pre_act = jnp.dot(chip_feats, w_first, preferred_element_type=f32)
    hidden = jax.nn.silu(pre_act).astype(bf16)
    restart = jnp.where(core == 0, ALPHA, 0.0).astype(f32)
    constant = restart * state.astype(f32)
    collected = state.astype(f32)
    for step in range(STEPS):
        if step == 0:
            parts = first_parts
        else:
            parts = [state] + [send(state, functools.partial(gather_ring, hop)) for hop in (1, 2, 3)]
        outs = block_product(meta, masks, tiles, parts)
        got = [outs[0]] + [send(outs[hop], functools.partial(scatter_ring, hop)) for hop in (1, 2, 3)]
        summed = sum(piece.astype(f32) for piece in got)
        state = ((1.0 - ALPHA) * summed + constant).astype(bf16)
        if step < STEPS - 1:
            collected = collected + state.astype(f32)
    last = jnp.where(core == 0, state, (ALPHA * collected + state.astype(f32)).astype(bf16))
    last = last.reshape(4, 8 * PACK, LANES)
    pieces = [last[0]] + [send(last[hop], functools.partial(z_move, -hop)) for hop in (1, 2, 3)]
    pieces = jnp.stack(pieces)[(jnp.arange(4) - spot) % 4]
    joined = join_features(pieces, core)
    ending = send(joined, core_move)
    propagated = jnp.where(core == 0, joined[:ITEMS], ending[ITEMS:])
    grad_teleport = jnp.where(core == 0, ending, joined)

    grad_hidden = lax.dot_general(
        grad_teleport, w_second, (((1,), (1,)), ((), ())), preferred_element_type=f32
    )
    grad_pre = (grad_hidden * silu_slope(pre_act)).astype(bf16)
    contract_items = (((0,), (0,)), ((), ()))
    first = lax.dot_general(chip_feats, grad_pre, contract_items, preferred_element_type=f32).astype(bf16)
    second = lax.dot_general(hidden, grad_teleport, contract_items, preferred_element_type=f32).astype(bf16)
    first = lax.dynamic_index_in_dim(first.reshape(8, 2, 16, 1024), core, 1, False)
    second = lax.dynamic_index_in_dim(second.reshape(8, 2, 64, 256), core, 1, False)
    first = first.reshape(8, 16, 2, 4, 128).transpose(2, 0, 3, 1, 4)
    second = second.reshape(8, 4, 16, 2, 128).transpose(3, 0, 1, 2, 4)
    spread = jnp.concatenate([first, second], axis=2).reshape(16, 128, 128)
    landed = lax.all_to_all(spread, ("zl", "zh", "x"), 0, 0)
    mine = jnp.sum(landed.astype(f32), axis=0).astype(bf16)
    shares = lax.all_to_all(jnp.broadcast_to(mine[None], (8, 128, 128)), LOOP, 0, 0)
    sums = jnp.sum(shares.reshape(2, 4, 8, 16, 128).astype(f32), axis=1)
    grad_first = sums[:, :4].transpose(2, 0, 1, 3).reshape(16, 1024)
    grad_second = sums[:, 4:].transpose(1, 2, 0, 3).reshape(64, 256)
    return (propagated[None], grad_first, grad_second)


def solution(mesh):
    fine = Mesh(mesh.devices.reshape(SIZES), AXES)
    return jax.shard_map(
        body,
        mesh=fine,
        in_specs=(
            P(WIDE, LOOP, None),
            P(),
            P(),
            P(WIDE, LOOP, None),
            P(LOOP, WIDE, None, None, None),
            P(LOOP, WIDE, None),
            P(LOOP, WIDE, None),
        ),
        out_specs=(P(WIDE, LOOP, None), P(WIDE, None), P(WIDE, None)),
        check_vma=False,
    )
```

```python
import functools

import jax
import jax.numpy as jnp
import numpy as np
from jax import lax
from jax.experimental import pallas as pl
from jax.experimental.pallas import tpu as pltpu
from jax.sharding import Mesh
from jax.sharding import PartitionSpec as P

STEPS = 3
ALPHA = 0.1
AXES = ("zl", "y", "zh", "x", "c")
SIZES = (2, 4, 2, 4, 2)
LOOP = ("zl", "y")
WIDE = ("zh", "x", "c")
BLK = 64
DIM = 256
ITEMS = 256
PIECE = 2 * ITEMS
SLOTS = 80
PACK = 32
LANES = 128
STATE = 1024
GRAPH = 4 * STATE
TILES = 8
GROUP = 64
LIST = TILES * SLOTS + GROUP


def permutation(move):
    pairs = []
    for source in range(int(np.prod(SIZES))):
        place = dict(zip(AXES, np.unravel_index(source, SIZES)))
        place = {name: int(value) for name, value in place.items()}
        place.update(move(place))
        pairs.append((source, int(np.ravel_multi_index([place[name] for name in AXES], SIZES))))
    return pairs


def send(value, move):
    return lax.ppermute(value, AXES, permutation(move))


def core_move(place):
    return {"c": 1 - place["c"]}


def z_move(step, place):
    spot = (2 * place["zh"] + place["zl"] + step) % 4
    return {"zh": spot // 2, "zl": spot % 2}


def relay_move(place):
    return z_move(3 if place["c"] else 1, place)


def gather_ring(step, place):
    return {"y": (place["y"] + step) % 4} if place["c"] else {"x": (place["x"] + step) % 4}


def scatter_ring(step, place):
    return {"x": (place["x"] + step) % 4} if place["c"] else {"y": (place["y"] + step) % 4}


def start_kernel(place, own, other, w_first, w_second, out):
    core, spot = place[0], place[1]
    for tile in range(2):
        rows = jnp.where(core == tile, own[...], other[...])
        pre_act = jnp.dot(rows[:ITEMS], w_first[...], preferred_element_type=jnp.float32)
        hidden = (pre_act / (1.0 + jnp.exp(-pre_act))).astype(jnp.bfloat16)
        teleport = jnp.dot(hidden, w_second[...], preferred_element_type=jnp.float32)
        straight = jnp.where(core == 0, teleport, rows[ITEMS:PIECE].astype(jnp.float32).T)
        for corner in range(4):
            pieces = []
            for block in range(4):
                low, high = block * BLK, corner * BLK
                first = jnp.where(core == 0, straight[low : low + BLK, high : high + BLK], straight[high : high + BLK, low : low + BLK])
                pieces.append(jnp.concatenate([first[:PACK], first[PACK:]], axis=1))
            spread = jnp.concatenate(pieces, axis=0).astype(jnp.bfloat16)
            out[(corner - spot) % 4, tile * ITEMS // 2 : (tile + 1) * ITEMS // 2, :] = spread
    for hop in range(4):
        out[hop, ITEMS : ITEMS + 16, :] = own[PIECE:, :LANES]
        out[hop, ITEMS + 16 :, :] = other[PIECE:, :LANES]


def start_pieces(place, own, other, w_first, w_second):
    return pl.pallas_call(
        start_kernel,
        out_shape=jax.ShapeDtypeStruct((4, 9 * PACK, LANES), jnp.bfloat16),
        in_specs=[pl.BlockSpec(memory_space=pltpu.SMEM)] + [pl.BlockSpec(memory_space=pltpu.VMEM)] * 4,
        out_specs=pl.BlockSpec(memory_space=pltpu.VMEM),
        compiler_params=pltpu.CompilerParams(vmem_limit_bytes=24 * 2**20),
        name="start_pieces",
    )(place, own, other, w_first, w_second)


def product_kernel(meta, masks, *refs):
    tiles, parts, outs = refs[:TILES], refs[TILES : TILES + 4], refs[TILES + 4 : TILES + 8]
    values, gathered, sums, sems = refs[TILES + 8 :]
    part_copies = [
        pltpu.make_async_copy(part, gathered.at[pl.ds(index * STATE, STATE)], sems.at[TILES + index])
        for index, part in enumerate(parts)
    ]
    tile_copies = [
        pltpu.make_async_copy(tile, values.at[pl.ds(index * SLOTS * PACK, SLOTS * PACK)], sems.at[index])
        for index, tile in enumerate(tiles)
    ]
    for copy in tile_copies[: TILES // 2] + part_copies + tile_copies[TILES // 2 :]:
        copy.start()
    sums[...] = jnp.zeros_like(sums)
    adjoint = meta[3, 2]
    left, right = masks[0], masks[1]

    def run(forward, begin, end):
        def group(index, carry):
            first = index * GROUP
            products = []
            for lane in range(GROUP):
                entries = values[pl.ds(pl.multiple_of(meta[2, first + lane], PACK), PACK), :]
                vectors = gathered[pl.ds(pl.multiple_of(meta[0, first + lane], PACK), PACK), :]
                rows, cols = (entries, vectors) if forward else (vectors, entries)
                turned = pltpu.roll(cols, BLK, 1)
                spread = jnp.concatenate([cols * left, turned * left, turned * right, cols * right], axis=0)
                products.append(jnp.dot(rows, spread, preferred_element_type=jnp.float32))
            for lane in range(GROUP):
                target = pl.multiple_of(meta[1, first + lane], PACK)
                sums[pl.ds(target, PACK), :] += products[lane]
            return carry

        lax.fori_loop(begin, end, group, 0)

    early = meta[3, 0] // GROUP
    total = (meta[3, 1] + GROUP - 1) // GROUP
    for copy in tile_copies[: TILES // 2] + part_copies:
        copy.wait()
    run(True, 0, jnp.where(adjoint == 0, early, 0))
    run(False, 0, jnp.where(adjoint == 0, 0, early))
    for copy in tile_copies[TILES // 2 :]:
        copy.wait()
    run(True, early, jnp.where(adjoint == 0, total, early))
    run(False, early, jnp.where(adjoint == 0, early, total))
    for index, out in enumerate(outs):
        out[...] = sums[index * STATE : (index + 1) * STATE, :].astype(out.dtype)


def block_product(meta, masks, tiles, parts):
    piece = jax.ShapeDtypeStruct((STATE, LANES), jnp.bfloat16)
    return pl.pallas_call(
        product_kernel,
        out_shape=(piece,) * 4,
        in_specs=[
            pl.BlockSpec(memory_space=pltpu.SMEM),
            pl.BlockSpec(memory_space=pltpu.VMEM),
        ]
        + [pl.BlockSpec(memory_space=pltpu.HBM)] * TILES
        + [pl.BlockSpec(memory_space=pl.ANY)] * 4,
        out_specs=(pl.BlockSpec(memory_space=pltpu.VMEM),) * 4,
        scratch_shapes=[
            pltpu.VMEM((TILES * SLOTS * PACK, LANES), jnp.bfloat16),
            pltpu.VMEM((GRAPH, LANES), jnp.bfloat16),
            pltpu.VMEM((GRAPH + PACK, LANES), jnp.float32),
            pltpu.SemaphoreType.DMA((TILES + 4,)),
        ],
        compiler_params=pltpu.CompilerParams(vmem_limit_bytes=20 * 2**20),
        name="block_product",
    )(meta, masks, *tiles, *parts)


def finish_kernel(place, own, other, feats, hidden, slope, w_second, spread, propagated):
    core, spot = place[0], place[1]
    f32, bf16 = jnp.float32, jnp.bfloat16
    strips, columns = [], []
    for corner in range(4):
        hop = (corner - spot) % 4
        piece = jnp.where(core == 1, own[hop], other[hop]).astype(f32)
        blocks = [piece[block * PACK : (block + 1) * PACK] for block in range(8)]
        top = jnp.concatenate([block[:, :BLK] for block in blocks], axis=1)
        bottom = jnp.concatenate([block[:, BLK:] for block in blocks], axis=1)
        strips += [top, bottom]
        rows = pl.ds(pl.multiple_of(core * 4 * PACK, 4 * PACK), 4 * PACK)
        piece = jnp.where(core == 0, own[hop, rows, :], other[hop, rows, :]).astype(f32)
        blocks = [piece[block * PACK : (block + 1) * PACK] for block in range(4)]
        columns.append(
            jnp.concatenate([half for block in blocks for half in (block[:, :BLK], block[:, BLK:])], axis=0)
        )
    propagated[...] = jnp.concatenate(columns, axis=1).astype(bf16)
    grad_teleport = jnp.concatenate(strips, axis=0).T.astype(bf16)
    grad_hidden = lax.dot_general(
        grad_teleport, w_second[...], (((1,), (1,)), ((), ())), preferred_element_type=f32
    )
    grad_pre = (grad_hidden * slope[...]).astype(bf16)
    first = jnp.dot(feats[...], grad_pre, preferred_element_type=f32).astype(bf16)
    second = jnp.dot(hidden[...], grad_teleport, preferred_element_type=f32).astype(bf16)
    for half in range(2):
        for owner in range(8):
            base = (half * 8 + owner) * LANES
            for part in range(4):
                spread[base + part * 16 : base + part * 16 + 16, :] = first[
                    owner * 16 : owner * 16 + 16, half * 512 + part * LANES : half * 512 + (part + 1) * LANES
                ]
            spread[base + BLK : base + 2 * BLK, :] = second[
                owner * BLK : (owner + 1) * BLK, half * LANES : (half + 1) * LANES
            ]


def finish(place, own, other, feats, hidden, slope, w_second):
    return pl.pallas_call(
        finish_kernel,
        out_shape=(
            jax.ShapeDtypeStruct((16 * LANES, LANES), jnp.bfloat16),
            jax.ShapeDtypeStruct((ITEMS, DIM), jnp.bfloat16),
        ),
        in_specs=[pl.BlockSpec(memory_space=pltpu.SMEM)] + [pl.BlockSpec(memory_space=pltpu.VMEM)] * 6,
        out_specs=(pl.BlockSpec(memory_space=pltpu.VMEM),) * 2,
        compiler_params=pltpu.CompilerParams(vmem_limit_bytes=24 * 2**20),
        name="finish",
    )(place, own, other, feats, hidden, slope, w_second)


def slot_tables(pointers, columns, zl, y, zh, x, core):
    slot_ids = jnp.arange(SLOTS, dtype=jnp.int32)
    rows = jnp.sum((pointers[:, 1:, None] <= slot_ids).astype(jnp.int32), axis=1)
    rows = jnp.minimum(rows, pointers.shape[1] - 2)
    live_count = pointers[:, -1]
    place = jnp.arange(TILES, dtype=jnp.int32)
    spot = 2 * zh + zl
    from_z = (spot - place) % 4
    tile_zh, tile_zl = (from_z // 2)[:, None], (from_z % 2)[:, None]
    tile_core = (core ^ (place // 4))[:, None]
    row_l = rows // 4
    row_y, row_z = row_l % 4, 2 * tile_zh + row_l // 4
    row_base = ((spot - row_z) % 4) * 8 + tile_core * 4 + rows % 4
    col_w = columns // 4
    col_x, col_z = (col_w // 2) % 4, 2 * (col_w // 8) + tile_zl
    col_base = ((spot - col_z) % 4) * 8 + (col_w % 2) * 4 + columns % 4
    forward_source = ((x - col_x) % 4) * STATE + col_base * PACK
    forward_target = ((row_y - y) % 4) * STATE + row_base * PACK
    adjoint_source = ((y - row_y) % 4) * STATE + row_base * PACK
    adjoint_target = ((col_x - x) % 4) * STATE + col_base * PACK
    source = jnp.where(core == 0, forward_source, adjoint_source)
    target = jnp.where(core == 0, forward_target, adjoint_target)
    codes = (source * (2 * GRAPH) + target).reshape(-1, 1)
    ends = jnp.cumsum(live_count)
    spots = jnp.arange(LIST, dtype=jnp.int32)
    passed = (spots[None, :] >= ends[:, None]).astype(jnp.int32)
    begin = jnp.sum(passed * live_count[:, None], axis=0)
    entry = jnp.minimum(jnp.sum(passed, axis=0), TILES - 1) * SLOTS + spots - begin
    hits = entry[None, :] == jnp.arange(TILES * SLOTS, dtype=jnp.int32)[:, None]
    codes = jnp.sum(jnp.where(hits, codes, 0), axis=0)
    listed = spots < ends[-1]
    source = jnp.where(listed, codes // (2 * GRAPH), 0)
    target = jnp.where(listed, codes % (2 * GRAPH), GRAPH)
    entry = jnp.where(listed, entry * PACK, 0)
    counts = jnp.where(spots == 0, ends[TILES // 2 - 1], jnp.where(spots == 1, ends[-1], core))
    return jnp.stack([source, target, entry, counts])


def pack_rows(blocks):
    return jnp.concatenate([blocks[..., :PACK, :], blocks[..., PACK:, :]], axis=-1)


def silu_slope(value):
    sigma = jax.nn.sigmoid(value)
    return sigma * (1.0 + value * (1.0 - sigma))


def by_tile(own, other, core):
    return jnp.where(core == 0, jnp.stack([own, other]), jnp.stack([other, own]))


def body(feats, w_first, w_second, cotangent, block_values, row_ptr, col_idx):
    f32, bf16 = jnp.float32, jnp.bfloat16
    zl, y, zh, x, core = (lax.axis_index(name) for name in AXES)
    spot = 2 * zh + zl
    table = jnp.concatenate([row_ptr[0, 0], col_idx[0, 0]]).astype(bf16)
    table = jnp.pad(table[None], ((0, 15), (0, DIM - 113)))
    message = jnp.concatenate([feats[0], cotangent[0], table])
    other = send(message, core_move)
    lanes = jnp.arange(LANES)
    masks = jnp.stack([lanes < BLK, lanes >= BLK]).astype(bf16)
    masks = jnp.broadcast_to(masks[:, None, :], (2, PACK, LANES))

    place = jnp.stack([core, spot])
    start = start_pieces(place, message, other, w_first, w_second)
    tile = pack_rows(block_values[0, 0]).reshape(SLOTS * PACK, LANES)
    own_swapped = send(tile, core_move)
    start, own_swapped = lax.optimization_barrier((start, own_swapped))
    start = [start[0]] + [send(start[hop], functools.partial(z_move, hop)) for hop in (1, 2, 3)]
    ahead = send(tile, functools.partial(z_move, 1))
    behind = send(tile, functools.partial(z_move, 3))
    start, ahead, behind = lax.optimization_barrier((start, ahead, behind))
    across = send(jnp.where(core == 0, ahead, behind), relay_move)
    state = jnp.concatenate([piece[:ITEMS] for piece in start])
    tables = jnp.stack([piece[ITEMS : ITEMS + PACK : 16] for piece in start]).astype(jnp.int32)
    tables = tables.transpose(1, 0, 2).reshape(TILES, LANES)
    meta = slot_tables(tables[:, :33], tables[:, 33:113], zl, y, zh, x, core)
    first_parts = [state] + [send(state, functools.partial(gather_ring, hop)) for hop in (1, 2, 3)]
    first_parts, across, meta = lax.optimization_barrier((first_parts, across, meta))
    same_core = [tile, ahead, across, behind]
    tiles = same_core + [own_swapped] + [send(piece, core_move) for piece in same_core[1:]]

    chip_feats = by_tile(message[:ITEMS], other[:ITEMS], core).reshape(PIECE, DIM)
    pre_act = jnp.dot(chip_feats, w_first, preferred_element_type=f32)
    hidden = jax.nn.silu(pre_act).astype(bf16)
    slope = silu_slope(pre_act)
    feats_rows = lax.dynamic_index_in_dim(chip_feats.T.reshape(8, 2, 16, PIECE), core, 1, False).reshape(128, PIECE)
    hidden_rows = lax.dynamic_index_in_dim(hidden.T.reshape(8, 2, 64, PIECE), core, 1, False).reshape(512, PIECE)
    restart = jnp.where(core == 0, ALPHA, 0.0).astype(f32)
    constant = restart * state.astype(f32)
    collected = state.astype(f32)
    for step in range(STEPS):
        if step == 0:
            parts = first_parts
        else:
            parts = [state] + [send(state, functools.partial(gather_ring, hop)) for hop in (1, 2, 3)]
        outs = block_product(meta, masks, tiles, parts)
        got = [outs[0]] + [send(outs[hop], functools.partial(scatter_ring, hop)) for hop in (1, 2, 3)]
        summed = sum(piece.astype(f32) for piece in got)
        state = ((1.0 - ALPHA) * summed + constant).astype(bf16)
        if step == 0:
            state, slope, feats_rows, hidden_rows = lax.optimization_barrier(
                (state, slope, feats_rows, hidden_rows)
            )
        if step < STEPS - 1:
            collected = collected + state.astype(f32)
    last = jnp.where(core == 0, state, (ALPHA * collected + state.astype(f32)).astype(bf16))
    last = last.reshape(4, 8 * PACK, LANES)
    pieces = jnp.stack([last[0]] + [send(last[hop], functools.partial(z_move, -hop)) for hop in (1, 2, 3)])
    spread, propagated = finish(
        place, pieces, send(pieces, core_move), feats_rows, hidden_rows, slope, w_second
    )
    spread = spread.reshape(16, LANES, LANES)
    landed = lax.all_to_all(spread, ("zl", "zh", "x"), 0, 0)
    mine = jnp.sum(landed.astype(f32), axis=0).astype(bf16)
    shares = lax.all_to_all(jnp.broadcast_to(mine[None], (8, 128, 128)), LOOP, 0, 0)
    sums = jnp.sum(shares.reshape(2, 4, 8, 16, 128).astype(f32), axis=1)
    grad_first = sums[:, :4].transpose(2, 0, 1, 3).reshape(16, 1024)
    grad_second = sums[:, 4:].transpose(1, 2, 0, 3).reshape(64, 256)
    return (propagated[None], grad_first, grad_second)


def solution(mesh):
    fine = Mesh(mesh.devices.reshape(SIZES), AXES)
    return jax.shard_map(
        body,
        mesh=fine,
        in_specs=(
            P(WIDE, LOOP, None),
            P(),
            P(),
            P(WIDE, LOOP, None),
            P(LOOP, WIDE, None, None, None),
            P(LOOP, WIDE, None),
            P(LOOP, WIDE, None),
        ),
        out_specs=(P(WIDE, LOOP, None), P(WIDE, None), P(WIDE, None)),
        check_vma=False,
    )
```

```python
import functools

import jax
import jax.numpy as jnp
import numpy as np
from jax import lax
from jax.experimental import pallas as pl
from jax.experimental.pallas import tpu as pltpu
from jax.sharding import Mesh
from jax.sharding import PartitionSpec as P

STEPS = 3
ALPHA = 0.1
AXES = ("zl", "y", "zh", "x", "c")
SIZES = (2, 4, 2, 4, 2)
LOOP = ("zl", "y")
WIDE = ("zh", "x", "c")
BLK = 64
DIM = 256
ITEMS = 256
PIECE = 2 * ITEMS
SLOTS = 80
PACK = 32
LANES = 128
STATE = 1024
GRAPH = 4 * STATE
TILES = 8
GROUP = 64
LIST = TILES * SLOTS + GROUP


def permutation(move):
    pairs = []
    for source in range(int(np.prod(SIZES))):
        place = dict(zip(AXES, np.unravel_index(source, SIZES)))
        place = {name: int(value) for name, value in place.items()}
        place.update(move(place))
        pairs.append((source, int(np.ravel_multi_index([place[name] for name in AXES], SIZES))))
    return pairs


def send(value, move):
    return lax.ppermute(value, AXES, permutation(move))


def core_move(place):
    return {"c": 1 - place["c"]}


def z_move(step, place):
    spot = (2 * place["zh"] + place["zl"] + step) % 4
    return {"zh": spot // 2, "zl": spot % 2}


def relay_move(place):
    return z_move(3 if place["c"] else 1, place)


def gather_ring(step, place):
    return {"y": (place["y"] + step) % 4} if place["c"] else {"x": (place["x"] + step) % 4}


def scatter_ring(step, place):
    return {"x": (place["x"] + step) % 4} if place["c"] else {"y": (place["y"] + step) % 4}


def start_kernel(place, own, other, w_first, w_second, out):
    core, spot = place[0], place[1]
    for tile in range(2):
        rows = jnp.where(core == tile, own[...], other[...])
        pre_act = jnp.dot(rows[:ITEMS], w_first[...], preferred_element_type=jnp.float32)
        hidden = (pre_act / (1.0 + jnp.exp(-pre_act))).astype(jnp.bfloat16)
        teleport = jnp.dot(hidden, w_second[...], preferred_element_type=jnp.float32)
        straight = jnp.where(core == 0, teleport, rows[ITEMS:PIECE].astype(jnp.float32).T)
        for corner in range(4):
            pieces = []
            for block in range(4):
                low, high = block * BLK, corner * BLK
                first = jnp.where(core == 0, straight[low : low + BLK, high : high + BLK], straight[high : high + BLK, low : low + BLK])
                pieces.append(jnp.concatenate([first[:PACK], first[PACK:]], axis=1))
            spread = jnp.concatenate(pieces, axis=0).astype(jnp.bfloat16)
            out[(corner - spot) % 4, tile * ITEMS // 2 : (tile + 1) * ITEMS // 2, :] = spread
    for hop in range(4):
        out[hop, ITEMS : ITEMS + 16, :] = own[PIECE:, :LANES]
        out[hop, ITEMS + 16 :, :] = other[PIECE:, :LANES]


def start_pieces(place, own, other, w_first, w_second):
    return pl.pallas_call(
        start_kernel,
        out_shape=jax.ShapeDtypeStruct((4, 9 * PACK, LANES), jnp.bfloat16),
        in_specs=[pl.BlockSpec(memory_space=pltpu.SMEM)] + [pl.BlockSpec(memory_space=pltpu.VMEM)] * 4,
        out_specs=pl.BlockSpec(memory_space=pltpu.VMEM),
        compiler_params=pltpu.CompilerParams(vmem_limit_bytes=24 * 2**20),
        name="start_pieces",
    )(place, own, other, w_first, w_second)


def product_kernel(meta, masks, *refs):
    tiles, parts, outs = refs[:TILES], refs[TILES : TILES + 4], refs[TILES + 4 : TILES + 8]
    values, gathered, sums, sems = refs[TILES + 8 :]
    part_copies = [
        pltpu.make_async_copy(part, gathered.at[pl.ds(index * STATE, STATE)], sems.at[TILES + index])
        for index, part in enumerate(parts)
    ]
    tile_copies = [
        pltpu.make_async_copy(tile, values.at[pl.ds(index * SLOTS * PACK, SLOTS * PACK)], sems.at[index])
        for index, tile in enumerate(tiles)
    ]
    for copy in tile_copies[: TILES // 2] + part_copies + tile_copies[TILES // 2 :]:
        copy.start()
    sums[...] = jnp.zeros_like(sums)
    adjoint = meta[3, 2]
    left, right = masks[0], masks[1]

    def run(forward, begin, end):
        def group(index, carry):
            first = index * GROUP
            products = []
            for lane in range(GROUP):
                entries = values[pl.ds(pl.multiple_of(meta[2, first + lane], PACK), PACK), :]
                vectors = gathered[pl.ds(pl.multiple_of(meta[0, first + lane], PACK), PACK), :]
                rows, cols = (entries, vectors) if forward else (vectors, entries)
                turned = pltpu.roll(cols, BLK, 1)
                spread = jnp.concatenate([cols * left, turned * left, turned * right, cols * right], axis=0)
                products.append(jnp.dot(rows, spread, preferred_element_type=jnp.float32))
            for lane in range(GROUP):
                target = pl.multiple_of(meta[1, first + lane], PACK)
                sums[pl.ds(target, PACK), :] += products[lane]
            return carry

        lax.fori_loop(begin, end, group, 0)

    early = meta[3, 0] // GROUP
    total = (meta[3, 1] + GROUP - 1) // GROUP
    for copy in tile_copies[: TILES // 2] + part_copies:
        copy.wait()
    run(True, 0, jnp.where(adjoint == 0, early, 0))
    run(False, 0, jnp.where(adjoint == 0, 0, early))
    for copy in tile_copies[TILES // 2 :]:
        copy.wait()
    run(True, early, jnp.where(adjoint == 0, total, early))
    run(False, early, jnp.where(adjoint == 0, early, total))
    for index, out in enumerate(outs):
        out[...] = sums[index * STATE : (index + 1) * STATE, :].astype(out.dtype)


def block_product(meta, masks, tiles, parts):
    piece = jax.ShapeDtypeStruct((STATE, LANES), jnp.bfloat16)
    return pl.pallas_call(
        product_kernel,
        out_shape=(piece,) * 4,
        in_specs=[
            pl.BlockSpec(memory_space=pltpu.SMEM),
            pl.BlockSpec(memory_space=pltpu.VMEM),
        ]
        + [pl.BlockSpec(memory_space=pltpu.HBM)] * TILES
        + [pl.BlockSpec(memory_space=pl.ANY)] * 4,
        out_specs=(pl.BlockSpec(memory_space=pltpu.VMEM),) * 4,
        scratch_shapes=[
            pltpu.VMEM((TILES * SLOTS * PACK, LANES), jnp.bfloat16),
            pltpu.VMEM((GRAPH, LANES), jnp.bfloat16),
            pltpu.VMEM((GRAPH + PACK, LANES), jnp.float32),
            pltpu.SemaphoreType.DMA((TILES + 4,)),
        ],
        compiler_params=pltpu.CompilerParams(vmem_limit_bytes=20 * 2**20),
        name="block_product",
    )(meta, masks, *tiles, *parts)


def finish_kernel(place, own, other, feats, hidden, slope, w_second, spread, propagated):
    core, spot = place[0], place[1]
    f32, bf16 = jnp.float32, jnp.bfloat16
    strips, columns = [], []
    for corner in range(4):
        hop = (corner - spot) % 4
        piece = jnp.where(core == 1, own[hop], other[hop]).astype(f32)
        blocks = [piece[block * PACK : (block + 1) * PACK] for block in range(8)]
        top = jnp.concatenate([block[:, :BLK] for block in blocks], axis=1)
        bottom = jnp.concatenate([block[:, BLK:] for block in blocks], axis=1)
        strips += [top, bottom]
        rows = pl.ds(pl.multiple_of(core * 4 * PACK, 4 * PACK), 4 * PACK)
        piece = jnp.where(core == 0, own[hop, rows, :], other[hop, rows, :]).astype(f32)
        blocks = [piece[block * PACK : (block + 1) * PACK] for block in range(4)]
        columns.append(
            jnp.concatenate([half for block in blocks for half in (block[:, :BLK], block[:, BLK:])], axis=0)
        )
    propagated[...] = jnp.concatenate(columns, axis=1).astype(bf16)
    grad_teleport = jnp.concatenate(strips, axis=0).T.astype(bf16)
    grad_hidden = lax.dot_general(
        grad_teleport, w_second[...], (((1,), (1,)), ((), ())), preferred_element_type=f32
    )
    grad_pre = (grad_hidden * slope[...]).astype(bf16)
    first = jnp.dot(feats[...], grad_pre, preferred_element_type=f32).astype(bf16)
    second = jnp.dot(hidden[...], grad_teleport, preferred_element_type=f32).astype(bf16)
    for half in range(2):
        for owner in range(8):
            base = (half * 8 + owner) * LANES
            for part in range(4):
                spread[base + part * 16 : base + part * 16 + 16, :] = first[
                    owner * 16 : owner * 16 + 16, half * 512 + part * LANES : half * 512 + (part + 1) * LANES
                ]
            spread[base + BLK : base + 2 * BLK, :] = second[
                owner * BLK : (owner + 1) * BLK, half * LANES : (half + 1) * LANES
            ]


def finish(place, own, other, feats, hidden, slope, w_second):
    return pl.pallas_call(
        finish_kernel,
        out_shape=(
            jax.ShapeDtypeStruct((16 * LANES, LANES), jnp.bfloat16),
            jax.ShapeDtypeStruct((ITEMS, DIM), jnp.bfloat16),
        ),
        in_specs=[pl.BlockSpec(memory_space=pltpu.SMEM)] + [pl.BlockSpec(memory_space=pltpu.VMEM)] * 6,
        out_specs=(pl.BlockSpec(memory_space=pltpu.VMEM),) * 2,
        compiler_params=pltpu.CompilerParams(vmem_limit_bytes=24 * 2**20),
        name="finish",
    )(place, own, other, feats, hidden, slope, w_second)


def slot_tables(pointers, columns, zl, y, zh, x, core):
    slot_ids = jnp.arange(SLOTS, dtype=jnp.int32)
    rows = jnp.sum((pointers[:, 1:, None] <= slot_ids).astype(jnp.int32), axis=1)
    rows = jnp.minimum(rows, pointers.shape[1] - 2)
    live_count = pointers[:, -1]
    place = jnp.arange(TILES, dtype=jnp.int32)
    spot = 2 * zh + zl
    from_z = (spot - place) % 4
    tile_zh, tile_zl = (from_z // 2)[:, None], (from_z % 2)[:, None]
    tile_core = (core ^ (place // 4))[:, None]
    row_l = rows // 4
    row_y, row_z = row_l % 4, 2 * tile_zh + row_l // 4
    row_base = ((spot - row_z) % 4) * 8 + tile_core * 4 + rows % 4
    col_w = columns // 4
    col_x, col_z = (col_w // 2) % 4, 2 * (col_w // 8) + tile_zl
    col_base = ((spot - col_z) % 4) * 8 + (col_w % 2) * 4 + columns % 4
    forward_source = ((x - col_x) % 4) * STATE + col_base * PACK
    forward_target = ((row_y - y) % 4) * STATE + row_base * PACK
    adjoint_source = ((y - row_y) % 4) * STATE + row_base * PACK
    adjoint_target = ((col_x - x) % 4) * STATE + col_base * PACK
    source = jnp.where(core == 0, forward_source, adjoint_source)
    target = jnp.where(core == 0, forward_target, adjoint_target)
    codes = (source * (2 * GRAPH) + target).reshape(-1, 1)
    ends = jnp.cumsum(live_count)
    spots = jnp.arange(LIST, dtype=jnp.int32)
    passed = (spots[None, :] >= ends[:, None]).astype(jnp.int32)
    begin = jnp.sum(passed * live_count[:, None], axis=0)
    entry = jnp.minimum(jnp.sum(passed, axis=0), TILES - 1) * SLOTS + spots - begin
    hits = entry[None, :] == jnp.arange(TILES * SLOTS, dtype=jnp.int32)[:, None]
    codes = jnp.sum(jnp.where(hits, codes, 0), axis=0)
    listed = spots < ends[-1]
    source = jnp.where(listed, codes // (2 * GRAPH), 0)
    target = jnp.where(listed, codes % (2 * GRAPH), GRAPH)
    entry = jnp.where(listed, entry * PACK, 0)
    counts = jnp.where(spots == 0, ends[TILES // 2 - 1], jnp.where(spots == 1, ends[-1], core))
    return jnp.stack([source, target, entry, counts])


def pack_rows(blocks):
    return jnp.concatenate([blocks[..., :PACK, :], blocks[..., PACK:, :]], axis=-1)


def silu_slope(value):
    sigma = jax.nn.sigmoid(value)
    return sigma * (1.0 + value * (1.0 - sigma))


def by_tile(own, other, core):
    return jnp.where(core == 0, jnp.stack([own, other]), jnp.stack([other, own]))


def body(feats, w_first, w_second, cotangent, block_values, row_ptr, col_idx):
    f32, bf16 = jnp.float32, jnp.bfloat16
    zl, y, zh, x, core = (lax.axis_index(name) for name in AXES)
    spot = 2 * zh + zl
    table = jnp.concatenate([row_ptr[0, 0], col_idx[0, 0]]).astype(bf16)
    table = jnp.pad(table[None], ((0, 15), (0, DIM - 113)))
    message = jnp.concatenate([feats[0], cotangent[0], table])
    other = send(message, core_move)
    lanes = jnp.arange(LANES)
    masks = jnp.stack([lanes < BLK, lanes >= BLK]).astype(bf16)
    masks = jnp.broadcast_to(masks[:, None, :], (2, PACK, LANES))

    place = jnp.stack([core, spot])
    start = start_pieces(place, message, other, w_first, w_second)
    tile = pack_rows(block_values[0, 0]).reshape(SLOTS * PACK, LANES)
    own_swapped = send(tile, core_move)
    start, own_swapped = lax.optimization_barrier((start, own_swapped))
    start = [start[0]] + [send(start[hop], functools.partial(z_move, hop)) for hop in (1, 2, 3)]
    ahead = send(tile, functools.partial(z_move, 1))
    behind = send(tile, functools.partial(z_move, 3))
    start, ahead, behind = lax.optimization_barrier((start, ahead, behind))
    far = jnp.where(core == 0, ahead, behind)
    far, start = lax.optimization_barrier((far, start))
    across = send(far, relay_move)
    state = jnp.concatenate([piece[:ITEMS] for piece in start])
    tables = jnp.stack([piece[ITEMS : ITEMS + PACK : 16] for piece in start]).astype(jnp.int32)
    tables = tables.transpose(1, 0, 2).reshape(TILES, LANES)
    meta = slot_tables(tables[:, :33], tables[:, 33:113], zl, y, zh, x, core)
    first_parts = [state] + [send(state, functools.partial(gather_ring, hop)) for hop in (1, 2, 3)]
    first_parts, across, meta = lax.optimization_barrier((first_parts, across, meta))
    same_core = [tile, ahead, across, behind]
    tiles = same_core + [own_swapped] + [send(piece, core_move) for piece in same_core[1:]]

    restart = jnp.where(core == 0, ALPHA, 0.0).astype(f32)
    constant = restart * state.astype(f32)
    collected = state.astype(f32)
    for step in range(STEPS):
        if step == 0:
            parts = first_parts
        else:
            parts = [state] + [send(state, functools.partial(gather_ring, hop)) for hop in (1, 2, 3)]
        outs = block_product(meta, masks, tiles, parts)
        if step == 0:
            outs, mlp_own, mlp_other = lax.optimization_barrier((outs, message[:ITEMS], other[:ITEMS]))
            chip_feats = by_tile(mlp_own, mlp_other, core).reshape(PIECE, DIM)
            pre_act = jnp.dot(chip_feats, w_first, preferred_element_type=f32)
            hidden = jax.nn.silu(pre_act).astype(bf16)
            slope = silu_slope(pre_act)
        if step == 1:
            outs, hidden, chip_feats = lax.optimization_barrier((outs, hidden, chip_feats))
            feats_rows = lax.dynamic_index_in_dim(chip_feats.T.reshape(8, 2, 16, PIECE), core, 1, False)
            hidden_rows = lax.dynamic_index_in_dim(hidden.T.reshape(8, 2, 64, PIECE), core, 1, False)
            feats_rows, hidden_rows = feats_rows.reshape(128, PIECE), hidden_rows.reshape(512, PIECE)
        got = [outs[0]] + [send(outs[hop], functools.partial(scatter_ring, hop)) for hop in (1, 2, 3)]
        summed = sum(piece.astype(f32) for piece in got)
        state = ((1.0 - ALPHA) * summed + constant).astype(bf16)
        if step == 0:
            state, slope, hidden, chip_feats = lax.optimization_barrier((state, slope, hidden, chip_feats))
        if step == 1:
            state, feats_rows, hidden_rows = lax.optimization_barrier((state, feats_rows, hidden_rows))
        if step < STEPS - 1:
            collected = collected + state.astype(f32)
    last = jnp.where(core == 0, state, (ALPHA * collected + state.astype(f32)).astype(bf16))
    last = last.reshape(4, 8 * PACK, LANES)
    pieces = jnp.stack([last[0]] + [send(last[hop], functools.partial(z_move, -hop)) for hop in (1, 2, 3)])
    spread, propagated = finish(
        place, pieces, send(pieces, core_move), feats_rows, hidden_rows, slope, w_second
    )
    spread = spread.reshape(16, LANES, LANES)
    landed = lax.all_to_all(spread, ("zl", "zh", "x"), 0, 0)
    mine = jnp.sum(landed.astype(f32), axis=0).astype(bf16)
    shares = lax.all_to_all(jnp.broadcast_to(mine[None], (8, 128, 128)), LOOP, 0, 0)
    sums = jnp.sum(shares.reshape(2, 4, 8, 16, 128).astype(f32), axis=1)
    grad_first = sums[:, :4].transpose(2, 0, 1, 3).reshape(16, 1024)
    grad_second = sums[:, 4:].transpose(1, 2, 0, 3).reshape(64, 256)
    return (propagated[None], grad_first, grad_second)


def solution(mesh):
    fine = Mesh(mesh.devices.reshape(SIZES), AXES)
    return jax.shard_map(
        body,
        mesh=fine,
        in_specs=(
            P(WIDE, LOOP, None),
            P(),
            P(),
            P(WIDE, LOOP, None),
            P(LOOP, WIDE, None, None, None),
            P(LOOP, WIDE, None),
            P(LOOP, WIDE, None),
        ),
        out_specs=(P(WIDE, LOOP, None), P(WIDE, None), P(WIDE, None)),
        check_vma=False,
    )
```

```python
import functools

import jax
import jax.numpy as jnp
import numpy as np
from jax import lax
from jax.experimental import pallas as pl
from jax.experimental.pallas import tpu as pltpu
from jax.sharding import Mesh
from jax.sharding import PartitionSpec as P

STEPS = 3
ALPHA = 0.1
AXES = ("zl", "y", "zh", "x", "c")
SIZES = (2, 4, 2, 4, 2)
LOOP = ("zl", "y")
WIDE = ("zh", "x", "c")
BLK = 64
DIM = 256
ITEMS = 256
PIECE = 2 * ITEMS
SLOTS = 80
PACK = 32
LANES = 128
STATE = 1024
GRAPH = 4 * STATE
TILES = 8
GROUP = 64
LIST = TILES * SLOTS + GROUP


def permutation(move):
    pairs = []
    for source in range(int(np.prod(SIZES))):
        place = dict(zip(AXES, np.unravel_index(source, SIZES)))
        place = {name: int(value) for name, value in place.items()}
        place.update(move(place))
        pairs.append((source, int(np.ravel_multi_index([place[name] for name in AXES], SIZES))))
    return pairs


def send(value, move):
    return lax.ppermute(value, AXES, permutation(move))


def core_move(place):
    return {"c": 1 - place["c"]}


def z_move(step, place):
    spot = (2 * place["zh"] + place["zl"] + step) % 4
    return {"zh": spot // 2, "zl": spot % 2}


def relay_move(place):
    return z_move(3 if place["c"] else 1, place)


def gather_ring(step, place):
    return {"y": (place["y"] + step) % 4} if place["c"] else {"x": (place["x"] + step) % 4}


def scatter_ring(step, place):
    return {"x": (place["x"] + step) % 4} if place["c"] else {"y": (place["y"] + step) % 4}


def start_kernel(place, own, other, w_first, w_second, out):
    core, spot = place[0], place[1]
    for tile in range(2):
        rows = jnp.where(core == tile, own[...], other[...])
        pre_act = jnp.dot(rows[:ITEMS], w_first[...], preferred_element_type=jnp.float32)
        hidden = (pre_act / (1.0 + jnp.exp(-pre_act))).astype(jnp.bfloat16)
        teleport = jnp.dot(hidden, w_second[...], preferred_element_type=jnp.float32)
        straight = jnp.where(core == 0, teleport, rows[ITEMS:PIECE].astype(jnp.float32).T)
        for corner in range(4):
            pieces = []
            for block in range(4):
                low, high = block * BLK, corner * BLK
                first = jnp.where(core == 0, straight[low : low + BLK, high : high + BLK], straight[high : high + BLK, low : low + BLK])
                pieces.append(jnp.concatenate([first[:PACK], first[PACK:]], axis=1))
            spread = jnp.concatenate(pieces, axis=0).astype(jnp.bfloat16)
            out[(corner - spot) % 4, tile * ITEMS // 2 : (tile + 1) * ITEMS // 2, :] = spread
    for hop in range(4):
        out[hop, ITEMS : ITEMS + 16, :] = own[PIECE:, :LANES]
        out[hop, ITEMS + 16 :, :] = other[PIECE:, :LANES]


def start_pieces(place, own, other, w_first, w_second):
    return pl.pallas_call(
        start_kernel,
        out_shape=jax.ShapeDtypeStruct((4, 9 * PACK, LANES), jnp.bfloat16),
        in_specs=[pl.BlockSpec(memory_space=pltpu.SMEM)] + [pl.BlockSpec(memory_space=pltpu.VMEM)] * 4,
        out_specs=pl.BlockSpec(memory_space=pltpu.VMEM),
        compiler_params=pltpu.CompilerParams(vmem_limit_bytes=24 * 2**20),
        name="start_pieces",
    )(place, own, other, w_first, w_second)


def product_kernel(meta, masks, *refs):
    tiles, parts, outs = refs[:TILES], refs[TILES : TILES + 4], refs[TILES + 4 : TILES + 8]
    values, gathered, sums, sems = refs[TILES + 8 :]
    part_copies = [
        pltpu.make_async_copy(part, gathered.at[pl.ds(index * STATE, STATE)], sems.at[TILES + index])
        for index, part in enumerate(parts)
    ]
    tile_copies = [
        pltpu.make_async_copy(tile, values.at[pl.ds(index * SLOTS * PACK, SLOTS * PACK)], sems.at[index])
        for index, tile in enumerate(tiles)
    ]
    for copy in tile_copies[: TILES // 2] + part_copies + tile_copies[TILES // 2 :]:
        copy.start()
    sums[...] = jnp.zeros_like(sums)
    adjoint = meta[3, 2]
    left, right = masks[0], masks[1]

    def run(forward, begin, end):
        def group(index, carry):
            first = index * GROUP
            products = []
            for lane in range(GROUP):
                entries = values[pl.ds(pl.multiple_of(meta[2, first + lane], PACK), PACK), :]
                vectors = gathered[pl.ds(pl.multiple_of(meta[0, first + lane], PACK), PACK), :]
                rows, cols = (entries, vectors) if forward else (vectors, entries)
                turned = pltpu.roll(cols, BLK, 1)
                spread = jnp.concatenate([cols * left, turned * left, turned * right, cols * right], axis=0)
                products.append(jnp.dot(rows, spread, preferred_element_type=jnp.float32))
            for lane in range(GROUP):
                target = pl.multiple_of(meta[1, first + lane], PACK)
                sums[pl.ds(target, PACK), :] += products[lane]
            return carry

        lax.fori_loop(begin, end, group, 0)

    early = meta[3, 0] // GROUP
    total = (meta[3, 1] + GROUP - 1) // GROUP
    for copy in tile_copies[: TILES // 2] + part_copies:
        copy.wait()
    run(True, 0, jnp.where(adjoint == 0, early, 0))
    run(False, 0, jnp.where(adjoint == 0, 0, early))
    for copy in tile_copies[TILES // 2 :]:
        copy.wait()
    run(True, early, jnp.where(adjoint == 0, total, early))
    run(False, early, jnp.where(adjoint == 0, early, total))
    for index, out in enumerate(outs):
        out[...] = sums[index * STATE : (index + 1) * STATE, :].astype(out.dtype)


def block_product(meta, masks, tiles, parts):
    piece = jax.ShapeDtypeStruct((STATE, LANES), jnp.bfloat16)
    return pl.pallas_call(
        product_kernel,
        out_shape=(piece,) * 4,
        in_specs=[
            pl.BlockSpec(memory_space=pltpu.SMEM),
            pl.BlockSpec(memory_space=pltpu.VMEM),
        ]
        + [pl.BlockSpec(memory_space=pltpu.HBM)] * TILES
        + [pl.BlockSpec(memory_space=pl.ANY)] * 4,
        out_specs=(pl.BlockSpec(memory_space=pltpu.VMEM),) * 4,
        scratch_shapes=[
            pltpu.VMEM((TILES * SLOTS * PACK, LANES), jnp.bfloat16),
            pltpu.VMEM((GRAPH, LANES), jnp.bfloat16),
            pltpu.VMEM((GRAPH + PACK, LANES), jnp.float32),
            pltpu.SemaphoreType.DMA((TILES + 4,)),
        ],
        compiler_params=pltpu.CompilerParams(vmem_limit_bytes=20 * 2**20),
        name="block_product",
    )(meta, masks, *tiles, *parts)


def finish_kernel(place, own, other, feats, hidden, slope, w_second, spread, propagated):
    core, spot = place[0], place[1]
    f32, bf16 = jnp.float32, jnp.bfloat16
    strips, columns = [], []
    for corner in range(4):
        hop = (corner - spot) % 4
        piece = jnp.where(core == 1, own[hop], other[hop]).astype(f32)
        blocks = [piece[block * PACK : (block + 1) * PACK] for block in range(8)]
        top = jnp.concatenate([block[:, :BLK] for block in blocks], axis=1)
        bottom = jnp.concatenate([block[:, BLK:] for block in blocks], axis=1)
        strips += [top, bottom]
        rows = pl.ds(pl.multiple_of(core * 4 * PACK, 4 * PACK), 4 * PACK)
        piece = jnp.where(core == 0, own[hop, rows, :], other[hop, rows, :]).astype(f32)
        blocks = [piece[block * PACK : (block + 1) * PACK] for block in range(4)]
        columns.append(
            jnp.concatenate([half for block in blocks for half in (block[:, :BLK], block[:, BLK:])], axis=0)
        )
    propagated[...] = jnp.concatenate(columns, axis=1).astype(bf16)
    grad_teleport = jnp.concatenate(strips, axis=0).T.astype(bf16)
    grad_hidden = lax.dot_general(
        grad_teleport, w_second[...], (((1,), (1,)), ((), ())), preferred_element_type=f32
    )
    grad_pre = (grad_hidden * slope[...]).astype(bf16)
    first = jnp.dot(feats[...], grad_pre, preferred_element_type=f32).astype(bf16)
    second = jnp.dot(hidden[...], grad_teleport, preferred_element_type=f32).astype(bf16)
    for half in range(2):
        for owner in range(8):
            base = (half * 8 + owner) * LANES
            for part in range(4):
                spread[base + part * 16 : base + part * 16 + 16, :] = first[
                    owner * 16 : owner * 16 + 16, half * 512 + part * LANES : half * 512 + (part + 1) * LANES
                ]
            spread[base + BLK : base + 2 * BLK, :] = second[
                owner * BLK : (owner + 1) * BLK, half * LANES : (half + 1) * LANES
            ]


def finish(place, own, other, feats, hidden, slope, w_second):
    return pl.pallas_call(
        finish_kernel,
        out_shape=(
            jax.ShapeDtypeStruct((16 * LANES, LANES), jnp.bfloat16),
            jax.ShapeDtypeStruct((ITEMS, DIM), jnp.bfloat16),
        ),
        in_specs=[pl.BlockSpec(memory_space=pltpu.SMEM)] + [pl.BlockSpec(memory_space=pltpu.VMEM)] * 6,
        out_specs=(pl.BlockSpec(memory_space=pltpu.VMEM),) * 2,
        compiler_params=pltpu.CompilerParams(vmem_limit_bytes=24 * 2**20),
        name="finish",
    )(place, own, other, feats, hidden, slope, w_second)


def slot_tables(pointers, columns, zl, y, zh, x, core):
    slot_ids = jnp.arange(SLOTS, dtype=jnp.int32)
    rows = jnp.sum((pointers[:, 1:, None] <= slot_ids).astype(jnp.int32), axis=1)
    rows = jnp.minimum(rows, pointers.shape[1] - 2)
    live_count = pointers[:, -1]
    place = jnp.arange(TILES, dtype=jnp.int32)
    spot = 2 * zh + zl
    from_z = (spot - place) % 4
    tile_zh, tile_zl = (from_z // 2)[:, None], (from_z % 2)[:, None]
    tile_core = (core ^ (place // 4))[:, None]
    row_l = rows // 4
    row_y, row_z = row_l % 4, 2 * tile_zh + row_l // 4
    row_base = ((spot - row_z) % 4) * 8 + tile_core * 4 + rows % 4
    col_w = columns // 4
    col_x, col_z = (col_w // 2) % 4, 2 * (col_w // 8) + tile_zl
    col_base = ((spot - col_z) % 4) * 8 + (col_w % 2) * 4 + columns % 4
    forward_source = ((x - col_x) % 4) * STATE + col_base * PACK
    forward_target = ((row_y - y) % 4) * STATE + row_base * PACK
    adjoint_source = ((y - row_y) % 4) * STATE + row_base * PACK
    adjoint_target = ((col_x - x) % 4) * STATE + col_base * PACK
    source = jnp.where(core == 0, forward_source, adjoint_source)
    target = jnp.where(core == 0, forward_target, adjoint_target)
    codes = (source * (2 * GRAPH) + target).reshape(-1, 1)
    ends = jnp.cumsum(live_count)
    spots = jnp.arange(LIST, dtype=jnp.int32)
    passed = (spots[None, :] >= ends[:, None]).astype(jnp.int32)
    begin = jnp.sum(passed * live_count[:, None], axis=0)
    entry = jnp.minimum(jnp.sum(passed, axis=0), TILES - 1) * SLOTS + spots - begin
    hits = entry[None, :] == jnp.arange(TILES * SLOTS, dtype=jnp.int32)[:, None]
    codes = jnp.sum(jnp.where(hits, codes, 0), axis=0)
    listed = spots < ends[-1]
    source = jnp.where(listed, codes // (2 * GRAPH), 0)
    target = jnp.where(listed, codes % (2 * GRAPH), GRAPH)
    entry = jnp.where(listed, entry * PACK, 0)
    counts = jnp.where(spots == 0, ends[TILES // 2 - 1], jnp.where(spots == 1, ends[-1], core))
    return jnp.stack([source, target, entry, counts])


def pack_rows(blocks):
    return jnp.concatenate([blocks[..., :PACK, :], blocks[..., PACK:, :]], axis=-1)


def silu_slope(value):
    sigma = jax.nn.sigmoid(value)
    return sigma * (1.0 + value * (1.0 - sigma))


def by_tile(own, other, core):
    return jnp.where(core == 0, jnp.stack([own, other]), jnp.stack([other, own]))


def body(feats, w_first, w_second, cotangent, block_values, row_ptr, col_idx):
    f32, bf16 = jnp.float32, jnp.bfloat16
    zl, y, zh, x, core = (lax.axis_index(name) for name in AXES)
    spot = 2 * zh + zl
    table = jnp.concatenate([row_ptr[0, 0], col_idx[0, 0]]).astype(bf16)
    table = jnp.pad(table[None], ((0, 15), (0, DIM - 113)))
    message = jnp.concatenate([feats[0], cotangent[0], table])
    other = send(message, core_move)
    lanes = jnp.arange(LANES)
    masks = jnp.stack([lanes < BLK, lanes >= BLK]).astype(bf16)
    masks = jnp.broadcast_to(masks[:, None, :], (2, PACK, LANES))

    place = jnp.stack([core, spot])
    start = start_pieces(place, message, other, w_first, w_second)
    tile = pack_rows(block_values[0, 0]).reshape(SLOTS * PACK, LANES)
    start = [start[0]] + [send(start[hop], functools.partial(z_move, hop)) for hop in (1, 2, 3)]
    ahead = send(tile, functools.partial(z_move, 1))
    behind = send(tile, functools.partial(z_move, 3))
    start, ahead, behind = lax.optimization_barrier((start, ahead, behind))
    far = jnp.where(core == 0, ahead, behind)
    far, start, near = lax.optimization_barrier((far, start, tile))
    across = send(far, relay_move)
    own_swapped = send(near, core_move)
    state = jnp.concatenate([piece[:ITEMS] for piece in start])
    tables = jnp.stack([piece[ITEMS : ITEMS + PACK : 16] for piece in start]).astype(jnp.int32)
    tables = tables.transpose(1, 0, 2).reshape(TILES, LANES)
    meta = slot_tables(tables[:, :33], tables[:, 33:113], zl, y, zh, x, core)
    first_parts = [state] + [send(state, functools.partial(gather_ring, hop)) for hop in (1, 2, 3)]
    first_parts, across, meta, own_swapped = lax.optimization_barrier((first_parts, across, meta, own_swapped))
    same_core = [tile, ahead, across, behind]
    tiles = same_core + [own_swapped] + [send(piece, core_move) for piece in same_core[1:]]

    restart = jnp.where(core == 0, ALPHA, 0.0).astype(f32)
    constant = restart * state.astype(f32)
    collected = state.astype(f32)
    for step in range(STEPS):
        if step == 0:
            parts = first_parts
        else:
            parts = [state] + [send(state, functools.partial(gather_ring, hop)) for hop in (1, 2, 3)]
        outs = block_product(meta, masks, tiles, parts)
        if step == 0:
            outs, mlp_own, mlp_other = lax.optimization_barrier((outs, message[:ITEMS], other[:ITEMS]))
            chip_feats = by_tile(mlp_own, mlp_other, core).reshape(PIECE, DIM)
            pre_act = jnp.dot(chip_feats, w_first, preferred_element_type=f32)
            hidden = jax.nn.silu(pre_act).astype(bf16)
            slope = silu_slope(pre_act)
        if step == 1:
            outs, hidden, chip_feats = lax.optimization_barrier((outs, hidden, chip_feats))
            feats_rows = lax.dynamic_index_in_dim(chip_feats.T.reshape(8, 2, 16, PIECE), core, 1, False)
            hidden_rows = lax.dynamic_index_in_dim(hidden.T.reshape(8, 2, 64, PIECE), core, 1, False)
            feats_rows, hidden_rows = feats_rows.reshape(128, PIECE), hidden_rows.reshape(512, PIECE)
        got = [outs[0]] + [send(outs[hop], functools.partial(scatter_ring, hop)) for hop in (1, 2, 3)]
        summed = sum(piece.astype(f32) for piece in got)
        state = ((1.0 - ALPHA) * summed + constant).astype(bf16)
        if step == 0:
            state, slope, hidden, chip_feats = lax.optimization_barrier((state, slope, hidden, chip_feats))
        if step == 1:
            state, feats_rows, hidden_rows = lax.optimization_barrier((state, feats_rows, hidden_rows))
        if step < STEPS - 1:
            collected = collected + state.astype(f32)
    last = jnp.where(core == 0, state, (ALPHA * collected + state.astype(f32)).astype(bf16))
    last = last.reshape(4, 8 * PACK, LANES)
    pieces = jnp.stack([last[0]] + [send(last[hop], functools.partial(z_move, -hop)) for hop in (1, 2, 3)])
    spread, propagated = finish(
        place, pieces, send(pieces, core_move), feats_rows, hidden_rows, slope, w_second
    )
    spread = spread.reshape(16, LANES, LANES)
    landed = lax.all_to_all(spread, ("zl", "zh", "x"), 0, 0)
    mine = jnp.sum(landed.astype(f32), axis=0).astype(bf16)
    shares = lax.all_to_all(jnp.broadcast_to(mine[None], (8, 128, 128)), LOOP, 0, 0)
    sums = jnp.sum(shares.reshape(2, 4, 8, 16, 128).astype(f32), axis=1)
    grad_first = sums[:, :4].transpose(2, 0, 1, 3).reshape(16, 1024)
    grad_second = sums[:, 4:].transpose(1, 2, 0, 3).reshape(64, 256)
    return (propagated[None], grad_first, grad_second)


def solution(mesh):
    fine = Mesh(mesh.devices.reshape(SIZES), AXES)
    return jax.shard_map(
        body,
        mesh=fine,
        in_specs=(
            P(WIDE, LOOP, None),
            P(),
            P(),
            P(WIDE, LOOP, None),
            P(LOOP, WIDE, None, None, None),
            P(LOOP, WIDE, None),
            P(LOOP, WIDE, None),
        ),
        out_specs=(P(WIDE, LOOP, None), P(WIDE, None), P(WIDE, None)),
        check_vma=False,
    )
```
